256 devices in a mesh: dp: 32 (over z, x), expert: 8 (over y, core).
Axes of the slice: x: 4, y: 4, z: 8, core: 2. Of those that a mesh axis runs over, the one named last changes fastest.
Arguments:
- grad_out: bfloat16 [32768, 1536], P(('dp', 'expert')), may hold values from -6 to 6
- expert_ids: int32 [32768, 2], P(('dp', 'expert')), may hold values from 0 to 7, all different within a row; in each aligned block of 128 rows (0 to 127, 128 to 255, ...) at most 48 rows name the same one
- gates: float32 [32768, 2], P(('dp', 'expert')), may hold values from 0.1 to 1
- routed_pre: bfloat16 [32, 8, 384, 3072], P('dp', 'expert'), may hold values from -6 to 6
- routed_down: bfloat16 [8, 3072, 1536], P('expert', 'dp'), may hold values from -0.109375 to 0.109375
- shared_pre: bfloat16 [32768, 6144], P('dp', 'expert'), may hold values from -6 to 6
- shared_down: bfloat16 [6144, 1536], P(('expert', 'dp')), may hold values from -0.078125 to 0.078125
Outputs:
- routed_pre_grad: bfloat16 [32, 8, 384, 3072], P('dp', 'expert')
- routed_down_grad: float32 [8, 3072, 1536], P('expert', 'dp')
- shared_pre_grad: bfloat16 [32768, 6144], P('dp', 'expert')
- shared_down_grad: float32 [6144, 1536], P(('expert', 'dp'))
- gate_grad: float32 [32768, 2], P(('dp', 'expert'))
The draws below stay inside these ranges and needn't reach their ends.
Inputs may be any that keep to these rules, and one draw needn't show every extreme that they name: `expert_ids`: each row names two different experts. Among the 128 rows of one device no expert is named more than 48 times, and in every draw some expert is named exactly 48 times by the rows of some device.
All inputs are finite; a program needn't handle non-finite values.
Results may differ from the reference program's by a relative error of at most 0.015.
Values may be sent and summed in bfloat16 or wider, within the bound.
No kernel may reach another device: no remote copies, remote signals or barrier semaphores. Data moves between devices by JAX's collectives and lax.ppermute only.
A program may use at most 128 MiB of HBM per device.

```python
import math
import jax
import jax.numpy as jnp
import numpy as np
from jax import lax

D = 1536
H = 3072
HS = 6144
TOK_DEV = 128
EXPERTS = 8
CAP = 48
SLOTS = 384
ROW_TOK = 1024
TOKENS = 32768
N_DP = 32
N_EXPERT = 8


def strengthened(array, rng, source, target, parts, factor):
    owner, partner = [(jnp.arange(array.shape[axis_at]) // (array.shape[axis_at] // parts)).reshape([-1 if axis == axis_at else 1 for axis in range(array.ndim)]) for axis_at in (source, target)]
    chosen = jax.random.permutation(rng, parts)[partner]
    strong = (owner == chosen) | (owner == (partner + parts // 2) % parts)
    return jnp.where(strong, factor * array, array)


def steps_of(own_key, shape, shards, least, largest):
    level = 1.0
    for dim, parts in shards:
        draws = jax.random.uniform(jax.random.fold_in(jax.random.fold_in(own_key, 6), dim), (parts,), jnp.float32, least / len(shards), largest / len(shards))
        level = level * jnp.repeat(jnp.exp(draws), shape[dim] // parts).reshape((-1,) + (1,) * (len(shape) - 1 - dim))
    return level


def deal_out(stream_key, own, number, rows, count, top, most, skew):
    sequence = jax.random.permutation(stream_key, count)
    heavy_load, usual = shares(count, rows * top, most, skew, True), shares(count, rows * top, most, skew, False)
    places = jnp.arange(count)

    def named(tallies, offset_by):
        used = int((tallies > 0).sum())
        fixed = max(1, used // 4)
        moved = fixed + (places - fixed + offset_by * (used - fixed)) % max(1, count - fixed)
        return jnp.zeros((count,), jnp.int32).at[sequence[jnp.where(places < fixed, places, moved)]].set(jnp.asarray(tallies, jnp.int32))

    tallies = jnp.where(number % 4 == 0, named(heavy_load, number // 4), named(usual, number - number // 4 - 1))
    mixed = jax.random.permutation(jax.random.fold_in(own, 3), count)
    donor, receiver = mixed[0:count // 2 * 2:2], mixed[1:count // 2 * 2:2]
    room = jnp.minimum(tallies[donor] - 1, most - tallies[receiver]) // 2
    room = jnp.where((donor == sequence[0]) | (receiver == sequence[0]) | (tallies[receiver] == 0), 0, jnp.maximum(room, 0))
    moved = jax.random.randint(jax.random.fold_in(own, 4), (count // 2,), 0, 1 << 20) % (room + 1)
    tallies = tallies.at[donor].add(-moved).at[receiver].add(moved)
    members = jnp.searchsorted(jnp.cumsum(tallies), jnp.arange(rows * top), side="right").astype(jnp.int32)
    listing = members.reshape(top, rows).T
    listing = listing[jax.random.permutation(jax.random.fold_in(own, 1), rows)]
    offset_by = jax.random.randint(jax.random.fold_in(own, 2), (rows, 1), 0, top)
    return jnp.take_along_axis(listing, (jnp.arange(top)[None, :] + offset_by) % top, axis=1)


def shares(number_of, total, limit, skew, full):
    weights = [(1 << 20) // math.isqrt(rank ** skew) + 1 for rank in range(1, number_of + 1)]
    largest = limit if full else min(limit, max(-(-total // number_of), total * weights[0] // sum(weights)))
    least = 1 if total - largest >= number_of - 1 else 0
    counts, surplus = [largest] + [least] * (number_of - 1), total - largest - least * (number_of - 1)
    while surplus > 0:
        candidates = [i for i in range(1, number_of) if counts[i] < largest] or [i for i in range(1, number_of) if counts[i] < limit]
        whole, budget = sum([weights[i] for i in candidates]), surplus
        for i in candidates:
            addition = min(limit - counts[i], max(1, budget * weights[i] // whole), surplus)
            counts[i] = counts[i] + addition
            surplus = surplus - addition
    return np.array(counts)


def gaussian(key, extent, deviation, bound, split=(), kind=jnp.bfloat16):
    factor_of = steps_of(key, extent, split, -0.22, 0.18) if split else 1.0
    result = jax.random.normal(key, extent, jnp.float32) * deviation * factor_of
    return jnp.minimum(jnp.maximum(result, -bound), bound).astype(kind)


def gaussian_with(key, dims, scale, limit, pieces, heavy, kind=jnp.bfloat16):
    result = scale * jax.random.normal(key, dims, jnp.float32)
    if pieces:
        result = result * steps_of(key, dims, pieces, -0.22, 0.18)
    return jnp.clip(strengthened(result, jax.random.fold_in(key, 3), *heavy), -limit, limit).astype(kind)


def setup_inputs(seed: int = 0) -> dict:
    key_list = jax.random.split(jax.random.key(seed), 8)
    grad_out = gaussian(key_list[0], (TOKENS, D), 1.0, 6.0, ((0, 256),))
    expert_ids_keys = jax.random.split(jax.random.fold_in(key_list[1], 1), TOKENS // TOK_DEV)
    expert_ids_turns = jax.random.permutation(jax.random.fold_in(key_list[1], 3), TOKENS // TOK_DEV)
    expert_ids = jax.vmap(lambda own, number: deal_out(jax.random.fold_in(key_list[1], 2), own, number, TOK_DEV, EXPERTS, 2, CAP, 2))(expert_ids_keys, expert_ids_turns).reshape((TOKENS, 2))
    gates = jnp.clip(0.1 + 0.9 * jax.random.uniform(key_list[2], (TOKENS, 2), jnp.float32) ** steps_of(key_list[2], (TOKENS, 2), ((0, 256),), -0.2, 0.2), 0.1, 1.0)
    routed_pre = gaussian_with(key_list[3], (N_DP, EXPERTS, SLOTS, H), 1.0, 6.0, ((0, 32), (1, 8)), (0, 3, 32, 2.75))
    routed_down = gaussian(key_list[4], (EXPERTS, H, D), H ** -0.5, 0.109375, ((0, 8), (1, 32)))
    shared_pre = gaussian_with(key_list[5], (TOKENS, HS), 1.0, 6.0, ((0, 32), (1, 8)), (0, 1, 32, 2.75))
    shared_down = gaussian(key_list[6], (HS, D), HS ** -0.5, 0.078125, ((0, 256),))
    return {"grad_out": grad_out, "expert_ids": expert_ids, "gates": gates, "routed_pre": routed_pre, "routed_down": routed_down, "shared_pre": shared_pre, "shared_down": shared_down}


SQRT_TWO_PI = 0.7978845608028654


def gelu_pair(inputs):
    cubic = inputs * inputs * inputs
    tangent = jnp.tanh(SQRT_TWO_PI * (inputs + 0.044715 * cubic))
    value = 0.5 * inputs * (1.0 + tangent)
    slope = 0.5 * (1.0 + tangent) + 0.5 * inputs * (1.0 - tangent * tangent) * SQRT_TWO_PI * (1.0 + 3.0 * 0.044715 * inputs * inputs)
    return value, slope


def slot_ranks(flat_ids, experts):
    labels = jnp.arange(experts, dtype=jnp.int32)
    onehot = (flat_ids[:, :, None] == labels[None, None, :]).astype(jnp.int32)
    before = jnp.cumsum(onehot, axis=1) - onehot
    return jnp.sum(before * onehot, axis=2).astype(jnp.int32)


def reference(grad_out, expert_ids, gates, routed_pre, routed_down, shared_pre, shared_down):
    blocks = TOKENS // TOK_DEV
    rank = slot_ranks(expert_ids.reshape(blocks, TOK_DEV * 2), EXPERTS)
    source = (jnp.arange(blocks, dtype=jnp.int32) % N_EXPERT)[:, None]
    slot = (source * CAP + rank).astype(jnp.int32).reshape(N_DP, ROW_TOK * 2)
    ids = expert_ids.reshape(N_DP, ROW_TOK * 2)
    gate_b = gates.astype(jnp.bfloat16).reshape(N_DP, ROW_TOK * 2)
    rows = grad_out.reshape(N_DP, ROW_TOK, D)
    shared_rows = shared_pre.reshape(N_DP, ROW_TOK, HS)
    routed_weight = routed_down.astype(jnp.float32)

    def step(totals, inputs):
        routed_total, shared_total = totals
        ids_d, slot_d, gate_d, rows_d, pre_d, spre_d = inputs
        twice = jnp.repeat(rows_d, 2, axis=0)
        routed_in = jnp.zeros((EXPERTS, SLOTS, D), jnp.bfloat16).at[ids_d, slot_d].set(twice)
        routed_gate = jnp.zeros((EXPERTS, SLOTS), jnp.bfloat16).at[ids_d, slot_d].set(gate_d)
        value, slope = gelu_pair(pre_d.astype(jnp.float32))
        hidden_b = value.astype(jnp.bfloat16)
        raw = jnp.einsum("esd,ehd->esh", routed_in.astype(jnp.float32), routed_weight)
        gate_col = routed_gate.astype(jnp.float32)[:, :, None]
        pre_grad = (gate_col * raw * slope).astype(jnp.bfloat16)
        score = jnp.sum(value * raw, axis=2)
        scaled = (gate_col * routed_in.astype(jnp.float32)).astype(jnp.bfloat16)
        term = jnp.einsum("esh,esd->ehd", hidden_b.astype(jnp.float32), scaled.astype(jnp.float32))
        term_b = lax.optimization_barrier(term.astype(jnp.bfloat16))
        routed_total = routed_total + term_b.astype(jnp.float32)
        gate_grad_d = score[ids_d, slot_d]
        svalue, sslope = gelu_pair(spre_d.astype(jnp.float32))
        shared_b = svalue.astype(jnp.bfloat16)
        raw_shared = jnp.dot(rows_d, shared_down.T, preferred_element_type=jnp.float32)
        spre_grad = (raw_shared * sslope).astype(jnp.bfloat16)
        sterm = jnp.dot(shared_b.T, rows_d, preferred_element_type=jnp.float32)
        sterm_b = lax.optimization_barrier(sterm.astype(jnp.bfloat16))
        shared_total = shared_total + sterm_b.astype(jnp.float32)
        return (routed_total, shared_total), (pre_grad, gate_grad_d, spre_grad)

    start = (jnp.zeros((EXPERTS, H, D), jnp.float32), jnp.zeros((HS, D), jnp.float32))
    totals, outputs = lax.scan(step, start, (ids, slot, gate_b, rows, routed_pre, shared_rows))
    routed_total, shared_total = totals
    pre_grads, gate_grads, spre_grads = outputs
    return pre_grads, routed_total, spre_grads.reshape(TOKENS, HS), shared_total, gate_grads.reshape(TOKENS, 2)
```

```python
import jax
import jax.numpy as jnp
from jax import lax
from jax.experimental import pallas as pl
from jax.experimental.pallas import tpu as pltpu
from jax.sharding import Mesh
from jax.sharding import PartitionSpec as P

DP = ("z", "x")
EXPERT = ("y", "c")
DP_EXPERT = ("z", "x", "y", "c")
EXPERT_DP = ("y", "c", "z", "x")
NZ, NX, NY, NC = 8, 4, 4, 2


SQRT_TWO_PI = 0.7978845608028654
BF = jnp.bfloat16
F32 = jnp.float32


def hop(a, axis, by):
    n = lax.axis_size(axis)
    return lax.ppermute(a, axis, [(i, (i + by) % n) for i in range(n)])


def gelu_pair(inputs):
    cubic = inputs * inputs * inputs
    tangent = jnp.tanh(SQRT_TWO_PI * (inputs + 0.044715 * cubic))
    value = 0.5 * inputs * (1.0 + tangent)
    slope = 0.5 * (1.0 + tangent) + 0.5 * inputs * (1.0 - tangent * tangent) * SQRT_TWO_PI * (
        1.0 + 3.0 * 0.044715 * inputs * inputs
    )
    return (value, slope)


def added(a, b):
    return (a.astype(F32) + b.astype(F32)).astype(BF)


def gather_four(a, axis, cut):
    first, second = cut(a)
    right = hop(a, axis, 1)
    left = hop(a, axis, -1)
    far_first = hop(cut(right)[0], axis, 1)
    far_second = hop(cut(left)[1], axis, -1)
    return a, right, (far_first, far_second), left


def gather_eight(a, axis, cut):
    right = [a]
    left = [a]
    for _ in range(3):
        right.append(hop(right[-1], axis, 1))
        left.append(hop(left[-1], axis, -1))
    far = (hop(cut(right[3])[0], axis, 1), hop(cut(left[3])[1], axis, -1))
    return right[0], right[1], right[2], right[3], far, left[3], left[2], left[1]


def cut_cols(a):
    half = a.shape[-1] // 2
    return a[..., :half], a[..., half:]


def cut_rows(a):
    half = a.shape[0] // 2
    return a[:half], a[half:]


def sum_ring(block, n, axis, cut, join):
    far_first, far_second = cut(block(n // 2))
    right = hop(far_first, axis, 1)
    left = hop(far_second, axis, -1)
    for r in range(n // 2 - 1, 0, -1):
        mine_r, mine_l = block(r), block(n - r)
        if r == n // 2 - 1:
            a, b = cut(mine_r)
            send_r = join(added(a, right), b)
            a, b = cut(mine_l)
            send_l = join(a, added(b, left))
        else:
            send_r = added(mine_r, right)
            send_l = added(mine_l, left)
        right = hop(send_r, axis, 1)
        left = hop(send_l, axis, -1)
    return block(0).astype(F32) + right.astype(F32) + left.astype(F32)


def join_cols(a, b):
    return jnp.concatenate([a, b], axis=-1)


def join_rows(a, b):
    return jnp.concatenate([a, b], axis=0)


def dispatch_kernel(sc, meta, *refs):
    pieces, (grp, recv, scal, gate) = refs[:10], refs[10:]
    owner, y, c = sc[0], sc[1], sc[2]
    blocks, width = meta.shape[0], meta.shape[2]
    tok = width
    half = tok // 2
    other = 1 - c

    def put(ref, dy, core, off):
        at = (2 * ((y + dy) % NY) + core) * tok + off
        grp[pl.ds(pl.multiple_of(at, half), ref.shape[0]), :] = ref[...]

    for base, core in ((0, c), (5, other)):
        put(pieces[base], 0, core, 0)
        put(pieces[base + 1], NY - 1, core, 0)
        put(pieces[base + 2], 1, core, 0)
        put(pieces[base + 3], 2, core, 0)
        put(pieces[base + 4], 2, core, half)

    me = owner.astype(F32)
    g0, g1, i0, i1 = meta[:, 0, :], meta[:, 1, :], meta[:, 2, :], meta[:, 3, :]
    hit0, hit1 = (i0 == me), (i1 == me)
    named = jnp.where(hit0 | hit1, 1.0, 0.0)
    picked = jnp.where(hit0, g0, jnp.where(hit1, g1, 0.0))
    earlier = lax.broadcasted_iota(jnp.int32, (tok, tok), 0)
    later = lax.broadcasted_iota(jnp.int32, (tok, tok), 1)
    tri = jnp.where(earlier < later, 1.0, 0.0).astype(BF)
    rank = lax.dot_general(
        named.astype(BF), tri, (((1,), (0,)), ((), ())), preferred_element_type=F32
    )
    rank = jnp.where(named > 0.0, rank, -1.0).astype(jnp.int32)
    cap = recv.shape[0] // blocks
    place = lax.broadcasted_iota(jnp.int32, (cap, tok), 0)
    for s in range(blocks):
        onehot = jnp.where(place == rank[s : s + 1, :], 1.0, 0.0)
        rows = lax.dot_general(
            onehot.astype(BF),
            grp[s * tok : (s + 1) * tok, :],
            (((1,), (0,)), ((), ())),
            preferred_element_type=F32,
        )
        weight = jnp.sum(onehot * picked[s : s + 1, :], axis=1, keepdims=True)
        recv[s * cap : (s + 1) * cap, :] = rows.astype(BF)
        scal[s * cap : (s + 1) * cap, :] = (weight * rows).astype(BF)
        gate[s * cap : (s + 1) * cap, :] = weight


def dispatch(scalars, meta, pieces, slots):
    tok, width = pieces[0].shape
    blocks = meta.shape[0]
    vm = pl.BlockSpec(memory_space=pltpu.VMEM)
    return pl.pallas_call(
        dispatch_kernel,
        name="dispatch",
        out_shape=(
            jax.ShapeDtypeStruct((blocks * tok, width), BF),
            jax.ShapeDtypeStruct((slots, width), BF),
            jax.ShapeDtypeStruct((slots, width), BF),
            jax.ShapeDtypeStruct((slots, 1), F32),
        ),
        in_specs=[pl.BlockSpec(memory_space=pltpu.SMEM)] + [vm] * 11,
        out_specs=(vm, vm, vm, vm),
        compiler_params=pltpu.CompilerParams(vmem_limit_bytes=32 << 20),
        cost_estimate=pl.CostEstimate(flops=200_000_000, bytes_accessed=10_000_000, transcendentals=0),
    )(scalars, meta, *pieces)


def terms_kernel(hidden, scal, tsh, ta, tb):
    out = lax.dot_general(
        hidden[...], scal[...], (((0,), (0,)), ((), ())), preferred_element_type=F32
    )
    nx, rows, half = ta.shape[1], hidden.shape[1] // ta.shape[1], ta.shape[3]
    out = out.astype(BF).reshape(nx, rows, 2 * half)
    ta[0, :, :rows, :] = out[:, :, :half]
    tb[0, :, :rows, :] = out[:, :, half:]
    ta[0, :, rows:, :] = tsh[0, :, :, :half]
    tb[0, :, rows:, :] = tsh[0, :, :, half:]


def terms(hidden, scal, tsh):
    slots, hid = hidden.shape
    width = scal.shape[1]
    rows, extra = hid // (NZ * NX), tsh.shape[2]
    shape = (NZ, NX, rows + extra, width // 2)
    out = jax.ShapeDtypeStruct(shape, BF)
    spec = pl.BlockSpec((1, *shape[1:]), lambda k: (k, 0, 0, 0))
    return pl.pallas_call(
        terms_kernel,
        name="terms",
        grid=(NZ,),
        out_shape=(out, out),
        in_specs=[
            pl.BlockSpec((slots, hid // NZ), lambda k: (0, k)),
            pl.BlockSpec((slots, width), lambda k: (0, 0)),
            pl.BlockSpec((1, NX, extra, width), lambda k: (k, 0, 0, 0)),
        ],
        out_specs=(spec, spec),
        compiler_params=pltpu.CompilerParams(vmem_limit_bytes=32 << 20),
        cost_estimate=pl.CostEstimate(
            flops=2 * slots * hid * width, bytes_accessed=18_000_000, transcendentals=0
        ),
    )(hidden, scal, tsh)


def raw_kernel(sc, *refs):
    *ins, out, wsh, score, whole, small = refs
    rows, gate, pre = ins[:3]
    own_a, right_a, far_a, left_a = ins[3:7]
    b_refs = ins[7:-2] if len(refs) > 0 else ()
    x = sc[1]
    n_rows = whole.shape[0] // NX
    extra = small.shape[0] // NX
    half = whole.shape[1] // 2

    def b_piece(xr):
        if len(b_refs) == 1:
            return b_refs[0], xr
        return b_refs[xr // 2], xr % 2

    for xr, ref in enumerate((own_a, right_a, far_a, left_a)):
        source = (x + (NX - xr)) % NX
        at = pl.multiple_of(source * n_rows, n_rows)
        sat = pl.multiple_of(source * extra, extra)
        b_ref, i = b_piece(xr)
        whole[pl.ds(at, n_rows), :half] = ref[0, :n_rows, :]
        whole[pl.ds(at, n_rows), half:] = b_ref[i, :n_rows, :]
        small[pl.ds(sat, extra), :half] = ref[0, n_rows:, :].astype(F32)
        small[pl.ds(sat, extra), half:] = b_ref[i, n_rows:, :].astype(F32)
    raw = lax.dot_general(
        rows[...], whole[...], (((1,), (1,)), ((), ())), preferred_element_type=F32
    )
    value, slope = gelu_pair(pre[...].astype(F32))
    out[...] = (gate[...] * raw * slope).astype(BF)
    score[...] = jnp.sum(value * raw, axis=1, keepdims=True)
    wsh[...] = small[...].astype(BF)


def raw_block(j, scalars, rows, gate, pre, a_pieces, b_piece, carried):
    slots, width = rows.shape
    hid = pre.shape[1]
    block = hid // NZ
    a_own, a_right, (a_first, a_second), a_left = a_pieces
    n_rows = block // NX
    extra = a_own.shape[1] - n_rows
    half = width // 2
    b_list = list(b_piece) if isinstance(b_piece, tuple) else [b_piece]
    far, far_at = (a_first, j) if j < NZ // 2 else (a_second, j - NZ // 2)

    def a_spec(at):
        return pl.BlockSpec((1, n_rows + extra, half), lambda i, sc: (at, 0, 0))

    in_specs = [
        pl.BlockSpec((slots, width), lambda i, sc: (0, 0)),
        pl.BlockSpec((slots, 1), lambda i, sc: (0, 0)),
        pl.BlockSpec((slots, block), lambda i, sc: (0, sc[0])),
        a_spec(j),
        a_spec(j),
        a_spec(far_at),
        a_spec(j),
    ]
    in_specs += [pl.BlockSpec(b.shape, lambda i, sc: (0, 0, 0)) for b in b_list]
    args = [rows, gate, pre, a_own, a_right, far, a_left, *b_list]
    aliases = {}
    in_specs += [pl.BlockSpec(memory_space=pl.ANY)] * 2
    if carried is not None:
        aliases = {1 + len(args): 0, 2 + len(args): 1}
        args += list(carried)
    else:
        args += [gate, gate]
    return pl.pallas_call(
        raw_kernel,
        name="raw",
        out_shape=(
            jax.ShapeDtypeStruct((slots, hid), BF),
            jax.ShapeDtypeStruct((NZ * NX * extra, width), BF),
            jax.ShapeDtypeStruct((slots, 1), F32),
        ),
        grid_spec=pltpu.PrefetchScalarGridSpec(
            num_scalar_prefetch=1,
            grid=(1,),
            in_specs=in_specs,
            out_specs=(
                pl.BlockSpec((slots, block), lambda i, sc: (0, sc[0])),
                pl.BlockSpec((NX * extra, width), lambda i, sc: (sc[0], 0)),
                pl.BlockSpec((slots, 1), lambda i, sc: (0, 0)),
            ),
            scratch_shapes=[pltpu.VMEM((block, width), BF), pltpu.VMEM((NX * extra, width), F32)],
        ),
        input_output_aliases=aliases,
        compiler_params=pltpu.CompilerParams(vmem_limit_bytes=32 << 20),
        cost_estimate=pl.CostEstimate(
            flops=2 * slots * block * width, bytes_accessed=5_000_000, transcendentals=slots * block
        ),
    )(scalars, *args)


def body(grad_out, expert_ids, gates, routed_pre, routed_down, shared_pre, shared_down):
    z, x, y, c = (lax.axis_index(a) for a in ("z", "x", "y", "c"))
    owner = y * NC + c
    n_exp = NY * NC
    tok, width = grad_out.shape
    slots = routed_pre.shape[2]
    cap = slots // n_exp
    half = width // 2

    metas = jnp.concatenate([gates.astype(BF).astype(F32).T, expert_ids.astype(F32).T], axis=0)
    metas = jnp.broadcast_to(metas[None], (n_exp, *metas.shape))
    metas = lax.all_to_all(metas, EXPERT, 0, 0, tiled=True)
    g_own, g_right, (g_far0, g_far1), g_left = gather_four(grad_out, "y", cut_rows)
    mine = (g_own, g_right, g_left, g_far0, g_far1)
    partner = tuple(hop(p, "c", 1) for p in mine)

    shard = jnp.concatenate([routed_down[0], shared_down], axis=0)
    a_shard, b_shard = shard[:, :half], shard[:, half:]
    za = gather_eight(a_shard, "z", cut_cols)
    za = jnp.stack([join_cols(*p) if isinstance(p, tuple) else p for p in za], axis=0)
    a_pieces = gather_four(za, "x", cut_rows)
    xb = gather_four(b_shard, "x", cut_cols)
    xb = jnp.stack([join_cols(*p) if isinstance(p, tuple) else p for p in xb], axis=0)
    b_pieces = gather_eight(xb, "z", cut_rows)

    pre = routed_pre[0, 0]
    hidden_b = gelu_pair(pre.astype(F32))[0].astype(BF)
    shared_b = gelu_pair(shared_pre.astype(F32))[0].astype(BF)

    scalars = jnp.stack([owner, y, c]).astype(jnp.int32)
    group_rows, recv_rows, scaled, gate_col = dispatch(scalars, metas, mine + partner, slots)

    shared_term = lax.dot_general(
        shared_b, group_rows, (((0,), (0,)), ((), ())), preferred_element_type=F32
    ).astype(BF)
    ta, tb = terms(hidden_b, scaled, shared_term.reshape(NZ, NX, -1, width))

    def along(t, dim, at):
        return lax.dynamic_index_in_dim(t, at, dim, keepdims=False)

    sum_a = sum_ring(lambda r: along(ta, 1, (x + r) % NX), NX, "x", cut_rows, join_rows).astype(BF)
    sum_b = sum_ring(lambda r: along(tb, 0, (z + r) % NZ), NZ, "z", cut_rows, join_rows).astype(BF)
    sum_a = sum_ring(lambda r: along(sum_a, 0, (z + r) % NZ), NZ, "z", cut_cols, join_cols)
    sum_b = sum_ring(lambda r: along(sum_b, 0, (x + r) % NX), NX, "x", cut_cols, join_cols)
    total = jnp.concatenate([sum_a, sum_b], axis=1)
    rows = routed_down.shape[1]

    carried, scores = None, []
    for j in range(NZ):
        sc = jnp.stack([(z + (NZ - j)) % NZ, x]).astype(jnp.int32)
        out, wsh, score = raw_block(j, sc, recv_rows, gate_col, pre, a_pieces, b_pieces[j], carried)
        carried = (out, wsh)
        scores.append(score)
    routed_pre_grad, whole_shared = carried
    slot_score = sum(scores[1:], scores[0])
    returned = lax.all_to_all(slot_score.reshape(n_exp, cap), EXPERT, 0, 0, tiled=True)

    labels = jnp.arange(n_exp, dtype=jnp.int32)
    onehot = expert_ids[:, :, None] == labels[None, None, :]
    named = jnp.any(onehot, axis=1).astype(F32)
    order = jnp.arange(tok, dtype=jnp.int32)
    tri = (order[None, :] < order[:, None]).astype(F32)
    counts = lax.dot_general(tri, named, (((1,), (0,)), ((), ())), preferred_element_type=F32)
    rank = jnp.sum(jnp.where(onehot, counts[:, None, :], 0.0), axis=2).astype(jnp.int32)
    slot = expert_ids * cap + rank
    each = jnp.arange(slots, dtype=jnp.int32)
    gate_grad = jnp.sum(
        jnp.where(slot[:, :, None] == each[None, None, :], returned.reshape(1, 1, slots), 0.0), axis=2
    )

    raw_shared = lax.dot_general(
        group_rows, whole_shared, (((1,), (1,)), ((), ())), preferred_element_type=F32
    )
    shared_pre_grad = (raw_shared * gelu_pair(shared_pre.astype(F32))[1]).astype(BF)
    return (
        routed_pre_grad.reshape(routed_pre.shape),
        total[:rows].reshape(1, rows, width),
        shared_pre_grad,
        total[rows:],
        gate_grad,
    )


def solution(mesh):
    split = Mesh(mesh.devices.reshape(NZ, NX, NY, NC), ("z", "x", "y", "c"))
    placed = (
        P(DP_EXPERT, None),
        P(DP_EXPERT, None),
        P(DP_EXPERT, None),
        P(DP, EXPERT, None, None),
        P(EXPERT, DP, None),
        P(DP, EXPERT),
        P(EXPERT_DP, None),
    )
    return jax.shard_map(
        body,
        mesh=split,
        in_specs=placed,
        out_specs=(
            P(DP, EXPERT, None, None),
            P(EXPERT, DP, None),
            P(DP, EXPERT),
            P(EXPERT_DP, None),
            P(DP_EXPERT, None),
        ),
        check_vma=False,
    )
```

```python
import jax
import jax.numpy as jnp
from jax import lax
from jax.experimental import pallas as pl
from jax.experimental.pallas import tpu as pltpu
from jax.sharding import Mesh
from jax.sharding import PartitionSpec as P


DP = ("z", "x")
EXPERT = ("y", "c")
DP_EXPERT = ("z", "x", "y", "c")
EXPERT_DP = ("y", "c", "z", "x")
NZ, NX, NY, NC = 8, 4, 4, 2


SQRT_TWO_PI = 0.7978845608028654
BF = jnp.bfloat16
F32 = jnp.float32


def hop(a, axis, by):
    n = lax.axis_size(axis)
    return lax.ppermute(a, axis, [(i, (i + by) % n) for i in range(n)])


def gelu_pair(inputs):
    cubic = inputs * inputs * inputs
    tangent = jnp.tanh(SQRT_TWO_PI * (inputs + 0.044715 * cubic))
    value = 0.5 * inputs * (1.0 + tangent)
    slope = 0.5 * (1.0 + tangent) + 0.5 * inputs * (1.0 - tangent * tangent) * SQRT_TWO_PI * (
        1.0 + 3.0 * 0.044715 * inputs * inputs
    )
    return (value, slope)


def added(a, b):
    return (a.astype(F32) + b.astype(F32)).astype(BF)


def gather_eight(a, axis, cut):
    right = [a]
    left = [a]
    for _ in range(1, 4):
        right.append(hop(right[-1], axis, 1))
        left.append(hop(left[-1], axis, -1))
    far = (hop(cut(right[3])[0], axis, 1), hop(cut(left[3])[1], axis, -1))
    return right[0], right[1], right[2], right[3], far, left[3], left[2], left[1]


def cut_rows(a):
    half = a.shape[0] // 2
    return a[:half], a[half:]


def sum_ring(block, n, axis, cut, join):
    far_first, far_second = cut(block(n // 2))
    right = hop(far_first, axis, 1)
    left = hop(far_second, axis, -1)
    for r in range(n // 2 - 1, 0, -1):
        mine_r, mine_l = block(r), block(n - r)
        if r == n // 2 - 1:
            a, b = cut(mine_r)
            send_r = join(added(a, right), b)
            a, b = cut(mine_l)
            send_l = join(a, added(b, left))
        else:
            send_r = added(mine_r, right)
            send_l = added(mine_l, left)
        right = hop(send_r, axis, 1)
        left = hop(send_l, axis, -1)
    return block(0).astype(F32) + right.astype(F32) + left.astype(F32)


def join_rows(a, b):
    return jnp.concatenate([a, b], axis=0)


def dispatch_kernel(sc, mine, partner, grp, recv, scal, gate):
    owner, core = sc[0], sc[1]
    tok, cap = grp.shape[0] // 2, recv.shape[0] // 2
    me = owner.astype(F32)
    earlier = lax.broadcasted_iota(jnp.int32, (tok, tok), 0)
    later = lax.broadcasted_iota(jnp.int32, (tok, tok), 1)
    tri = jnp.where(earlier < later, 1.0, 0.0).astype(BF)
    place = lax.broadcasted_iota(jnp.int32, (cap, tok), 0)
    for ref, at in ((mine, core), (partner, 1 - core)):
        tokens = ref[0, :tok, :]
        meta = ref[0, tok:, :tok].astype(F32)
        g0, g1, i0, i1 = (meta[k : k + 1, :] for k in range(4))
        hit0, hit1 = (i0 == me), (i1 == me)
        named = jnp.where(hit0, 1.0, jnp.where(hit1, 1.0, 0.0))
        picked = jnp.where(hit0, g0, jnp.where(hit1, g1, 0.0))
        rank = lax.dot_general(
            jnp.broadcast_to(named, (8, tok)).astype(BF),
            tri,
            (((1,), (0,)), ((), ())),
            preferred_element_type=F32,
        )[0:1]
        rank = jnp.where(named > 0.0, rank, -1.0).astype(jnp.int32)
        onehot = jnp.where(place == rank, 1.0, 0.0)
        rows = lax.dot_general(
            onehot.astype(BF), tokens, (((1,), (0,)), ((), ())), preferred_element_type=F32
        )
        weight = jnp.sum(onehot * picked, axis=1, keepdims=True)
        grp[pl.ds(pl.multiple_of(at * tok, tok), tok), :] = tokens
        slot = pl.ds(pl.multiple_of(at * cap, cap), cap)
        recv[slot, :] = rows.astype(BF)
        scal[slot, :] = (weight * rows).astype(BF)
        gate[slot, :] = weight


def dispatch(scalars, mine, partner, tok, slots):
    width = mine.shape[2]
    cap2 = slots // NY
    taken = pl.BlockSpec((1, *mine.shape[1:]), lambda k: (k, 0, 0))

    def given(rows, cols):
        return pl.BlockSpec((rows, cols), lambda k: (k, 0))

    return pl.pallas_call(
        dispatch_kernel,
        name="dispatch",
        grid=(NY,),
        out_shape=(
            jax.ShapeDtypeStruct((NY * NC * tok, width), BF),
            jax.ShapeDtypeStruct((slots, width), BF),
            jax.ShapeDtypeStruct((slots, width), BF),
            jax.ShapeDtypeStruct((slots, 1), F32),
        ),
        in_specs=[pl.BlockSpec(memory_space=pltpu.SMEM), taken, taken],
        out_specs=(given(NC * tok, width), given(cap2, width), given(cap2, width), given(cap2, 1)),
        compiler_params=pltpu.CompilerParams(vmem_limit_bytes=24 << 20),
        cost_estimate=pl.CostEstimate(flops=200_000_000, bytes_accessed=10_000_000, transcendentals=0),
    )(scalars, mine, partner)


def terms_kernel(hidden, scal, tsh, ta, tb):
    out = lax.dot_general(
        hidden[...], scal[...], (((0,), (0,)), ((), ())), preferred_element_type=F32
    )
    nx, rows, half = tb.shape[1], hidden.shape[1] // tb.shape[1], tb.shape[3]
    out = out.astype(BF).reshape(nx, rows, 2 * half)
    ta[:, 0, :rows, :] = out[:, :, :half]
    tb[0, :, :rows, :] = out[:, :, half:]
    ta[:, 0, rows:, :] = tsh[0, :, :, :half]
    tb[0, :, rows:, :] = tsh[0, :, :, half:]


def terms(hidden, scal, tsh):
    slots, hid = hidden.shape
    width = scal.shape[1]
    rows, extra = hid // (NZ * NX), tsh.shape[2]
    tail = (rows + extra, width // 2)
    return pl.pallas_call(
        terms_kernel,
        name="terms",
        grid=(NZ,),
        out_shape=(
            jax.ShapeDtypeStruct((NX, NZ, *tail), BF),
            jax.ShapeDtypeStruct((NZ, NX, *tail), BF),
        ),
        in_specs=[
            pl.BlockSpec((slots, hid // NZ), lambda k: (0, k)),
            pl.BlockSpec((slots, width), lambda k: (0, 0)),
            pl.BlockSpec((1, NX, extra, width), lambda k: (k, 0, 0, 0)),
        ],
        out_specs=(
            pl.BlockSpec((NX, 1, *tail), lambda k: (0, k, 0, 0)),
            pl.BlockSpec((1, NX, *tail), lambda k: (k, 0, 0, 0)),
        ),
        compiler_params=pltpu.CompilerParams(vmem_limit_bytes=24 << 20),
        cost_estimate=pl.CostEstimate(
            flops=2 * slots * hid * width, bytes_accessed=18_000_000, transcendentals=0
        ),
    )(hidden, scal, tsh)


RAW_STEPS = 3
ARRIVAL = (0, 1, 7, 2, 6, 3, 5, 4)


def raw_kernel(sc, rows, gate, pre, a_ref, *refs):
    *b_refs, _, _, out, wsh, score, whole, small = refs
    n_rows = whole.shape[0] // NX
    extra = small.shape[0] // NX
    half = whole.shape[1] // 2

    @pl.when(pl.program_id(0) == 0)
    def _():
        for k in range(NX):
            b_ref, i = (b_refs[0], k) if len(b_refs) == 1 else (b_refs[k // 2], k % 2)
            whole[k * n_rows : (k + 1) * n_rows, :half] = a_ref[k, 0, :n_rows, :]
            whole[k * n_rows : (k + 1) * n_rows, half:] = b_ref[i, :n_rows, :]
            small[k * extra : (k + 1) * extra, :half] = a_ref[k, 0, n_rows:, :].astype(F32)
            small[k * extra : (k + 1) * extra, half:] = b_ref[i, n_rows:, :].astype(F32)
        wsh[...] = small[...].astype(BF)

    raw = lax.dot_general(
        rows[...], whole[...], (((1,), (1,)), ((), ())), preferred_element_type=F32
    )
    value, slope = gelu_pair(pre[...].astype(F32))
    out[...] = (gate[...] * raw * slope).astype(BF)
    score[...] = jnp.sum(value * raw, axis=1, keepdims=True)


def raw_block(scalars, rows, gate, pre, a_whole, b_piece, carried):
    slots, width = rows.shape
    hid = pre.shape[1]
    block, step = hid // NZ, slots // RAW_STEPS
    n_rows = block // NX
    extra = a_whole.shape[2] - n_rows
    half = width // 2
    b_list = list(b_piece) if isinstance(b_piece, tuple) else [b_piece]
    in_specs = [
        pl.BlockSpec((step, width), lambda i, sc: (i, 0)),
        pl.BlockSpec((step, 1), lambda i, sc: (i, 0)),
        pl.BlockSpec((step, block), lambda i, sc: (i, sc[0])),
        pl.BlockSpec((NX, 1, n_rows + extra, half), lambda i, sc: (0, sc[0], 0, 0)),
    ]
    in_specs += [pl.BlockSpec(b.shape, lambda i, sc: (0, 0, 0)) for b in b_list]
    args = [rows, gate, pre, a_whole, *b_list]
    aliases = {}
    in_specs += [pl.BlockSpec(memory_space=pl.ANY)] * 2
    if carried is not None:
        aliases = {1 + len(args): 0, 2 + len(args): 1}
        args += list(carried)
    else:
        args += [gate, gate]
    return pl.pallas_call(
        raw_kernel,
        name="raw",
        out_shape=(
            jax.ShapeDtypeStruct((slots, hid), BF),
            jax.ShapeDtypeStruct((NZ * NX * extra, width), BF),
            jax.ShapeDtypeStruct((slots, 1), F32),
        ),
        grid_spec=pltpu.PrefetchScalarGridSpec(
            num_scalar_prefetch=1,
            grid=(RAW_STEPS,),
            in_specs=in_specs,
            out_specs=(
                pl.BlockSpec((step, block), lambda i, sc: (i, sc[0])),
                pl.BlockSpec((NX * extra, width), lambda i, sc: (sc[0], 0)),
                pl.BlockSpec((step, 1), lambda i, sc: (i, 0)),
            ),
            scratch_shapes=[pltpu.VMEM((block, width), BF), pltpu.VMEM((NX * extra, width), F32)],
        ),
        input_output_aliases=aliases,
        compiler_params=pltpu.CompilerParams(vmem_limit_bytes=16 << 20),
        cost_estimate=pl.CostEstimate(
            flops=2 * slots * block * width, bytes_accessed=5_000_000, transcendentals=slots * block
        ),
    )(scalars, *args)


def to_all(a, axis, n):
    many = jnp.broadcast_to(a[None], (n, *a.shape))
    return lax.all_to_all(many, axis, 0, 0, tiled=True)


def body(grad_out, expert_ids, gates, routed_pre, routed_down, shared_pre, shared_down):
    z, _, y, c = (lax.axis_index(a) for a in ("z", "x", "y", "c"))
    owner = y * NC + c
    n_exp = NY * NC
    tok, width = grad_out.shape
    slots = routed_pre.shape[2]
    cap = slots // n_exp
    half = width // 2

    shard = jnp.concatenate([routed_down[0], shared_down], axis=0)
    a_whole = lax.all_gather(shard[:, :half], "z")
    a_whole = lax.all_gather(a_whole, "x")
    b_pieces = gather_eight(to_all(shard[:, half:], "x", NX), "z", cut_rows)

    metas = jnp.concatenate([gates.astype(BF).T, expert_ids.astype(BF).T], axis=0)
    metas = jnp.pad(metas, ((0, 8 - metas.shape[0]), (0, width - tok)))
    mine = to_all(jnp.concatenate([grad_out, metas], axis=0), "y", NY)
    partner = hop(mine, "c", 1)

    pre = routed_pre[0, 0]
    hidden_b = gelu_pair(pre.astype(F32))[0].astype(BF)
    shared_b = gelu_pair(shared_pre.astype(F32))[0].astype(BF)

    scalars = jnp.stack([owner, c]).astype(jnp.int32)
    group_rows, recv_rows, scaled, gate_col = dispatch(scalars, mine, partner, tok, slots)

    shared_term = lax.dot_general(
        shared_b, group_rows, (((0,), (0,)), ((), ())), preferred_element_type=F32
    ).astype(BF)
    ta, tb = terms(hidden_b, scaled, shared_term.reshape(NZ, NX, -1, width))
    sum_a = lax.psum_scatter(ta.reshape(-1, half), "x", scatter_dimension=0, tiled=True)
    sum_a = lax.psum_scatter(sum_a, "z", scatter_dimension=0, tiled=True)
    sum_a = sum_a.astype(F32)

    def along(r):
        return lax.dynamic_index_in_dim(tb, (z + r) % NZ, 0, keepdims=False)

    sum_b = sum_ring(along, NZ, "z", cut_rows, join_rows).astype(BF)
    sum_b = lax.all_to_all(sum_b, "x", 0, 0, tiled=True).astype(F32).sum(axis=0)
    total = jnp.concatenate([sum_a, sum_b], axis=1)
    rows = routed_down.shape[1]

    carried, scores = None, []
    for j in ARRIVAL:
        sc = jnp.stack([(z + (NZ - j)) % NZ]).astype(jnp.int32)
        out, wsh, score = raw_block(sc, recv_rows, gate_col, pre, a_whole, b_pieces[j], carried)
        carried = (out, wsh)
        scores.append(score)
    routed_pre_grad, whole_shared = carried
    slot_score = sum(scores[1:], scores[0])
    returned = lax.all_to_all(slot_score.reshape(n_exp, cap), EXPERT, 0, 0, tiled=True)

    labels = jnp.arange(n_exp, dtype=jnp.int32)
    onehot = expert_ids[:, :, None] == labels[None, None, :]
    named = jnp.any(onehot, axis=1).astype(F32)
    order = jnp.arange(tok, dtype=jnp.int32)
    tri = (order[None, :] < order[:, None]).astype(F32)
    counts = lax.dot_general(tri, named, (((1,), (0,)), ((), ())), preferred_element_type=F32)
    rank = jnp.sum(jnp.where(onehot, counts[:, None, :], 0.0), axis=2).astype(jnp.int32)
    slot = expert_ids * cap + rank
    each = jnp.arange(slots, dtype=jnp.int32)
    gate_grad = jnp.sum(
        jnp.where(slot[:, :, None] == each[None, None, :], returned.reshape(1, 1, slots), 0.0), axis=2
    )

    raw_shared = lax.dot_general(
        group_rows, whole_shared, (((1,), (1,)), ((), ())), preferred_element_type=F32
    )
    shared_pre_grad = (raw_shared * gelu_pair(shared_pre.astype(F32))[1]).astype(BF)
    return (
        routed_pre_grad.reshape(routed_pre.shape),
        total[:rows].reshape(1, rows, width),
        shared_pre_grad,
        total[rows:],
        gate_grad,
    )


def solution(mesh):
    split = Mesh(mesh.devices.reshape(NZ, NX, NY, NC), ("z", "x", "y", "c"))
    placed = (
        P(DP_EXPERT, None),
        P(DP_EXPERT, None),
        P(DP_EXPERT, None),
        P(DP, EXPERT, None, None),
        P(EXPERT, DP, None),
        P(DP, EXPERT),
        P(EXPERT_DP, None),
    )
    return jax.shard_map(
        body,
        mesh=split,
        in_specs=placed,
        out_specs=(
            P(DP, EXPERT, None, None),
            P(EXPERT, DP, None),
            P(DP, EXPERT),
            P(EXPERT_DP, None),
            P(DP_EXPERT, None),
        ),
        check_vma=False,
    )
```

```python
import functools

import jax
import jax.numpy as jnp
from jax import lax
from jax.experimental import pallas as pl
from jax.experimental.pallas import tpu as pltpu
from jax.sharding import Mesh
from jax.sharding import PartitionSpec as P


DP = ("z", "x")
EXPERT = ("y", "c")
DP_EXPERT = ("z", "x", "y", "c")
EXPERT_DP = ("y", "c", "z", "x")
NZ, NX, NY, NC = 8, 4, 4, 2


SQRT_TWO_PI = 0.7978845608028654
BF = jnp.bfloat16
F32 = jnp.float32


def hop(a, axis, by):
    n = lax.axis_size(axis)
    return lax.ppermute(a, axis, [(i, (i + by) % n) for i in range(n)])


def gelu_pair(inputs):
    cubic = inputs * inputs * inputs
    tangent = jnp.tanh(SQRT_TWO_PI * (inputs + 0.044715 * cubic))
    value = 0.5 * inputs * (1.0 + tangent)
    slope = 0.5 * (1.0 + tangent) + 0.5 * inputs * (1.0 - tangent * tangent) * SQRT_TWO_PI * (
        1.0 + 3.0 * 0.044715 * inputs * inputs
    )
    return (value, slope)


def added(a, b):
    return (a.astype(F32) + b.astype(F32)).astype(BF)


def gather_eight(a, axis, cut):
    right = [a]
    left = [a]
    for _ in range(1, 4):
        right.append(hop(right[-1], axis, 1))
        left.append(hop(left[-1], axis, -1))
    far = (hop(cut(right[3])[0], axis, 1), hop(cut(left[3])[1], axis, -1))
    return right[0], right[1], right[2], right[3], far, left[3], left[2], left[1]


def cut_rows(a):
    half = a.shape[0] // 2
    return a[:half], a[half:]


def sum_ring(block, n, axis, cut, join):
    far_first, far_second = cut(block(n // 2))
    right = hop(far_first, axis, 1)
    left = hop(far_second, axis, -1)
    for r in range(n // 2 - 1, 0, -1):
        mine_r, mine_l = block(r), block(n - r)
        if r == n // 2 - 1:
            a, b = cut(mine_r)
            send_r = join(added(a, right), b)
            a, b = cut(mine_l)
            send_l = join(a, added(b, left))
        else:
            send_r = added(mine_r, right)
            send_l = added(mine_l, left)
        right = hop(send_r, axis, 1)
        left = hop(send_l, axis, -1)
    return block(0).astype(F32) + right.astype(F32) + left.astype(F32)


def join_rows(a, b):
    return jnp.concatenate([a, b], axis=0)


def dispatch_kernel(sc, mine, partner, grp, recv, scal, gate):
    owner, core = sc[0], sc[1]
    tok, cap = grp.shape[0] // 2, recv.shape[0] // 2
    me = owner.astype(F32)
    earlier = lax.broadcasted_iota(jnp.int32, (tok, tok), 0)
    later = lax.broadcasted_iota(jnp.int32, (tok, tok), 1)
    tri = jnp.where(earlier < later, 1.0, 0.0).astype(BF)
    place = lax.broadcasted_iota(jnp.int32, (cap, tok), 0)
    for ref, at in ((mine, core), (partner, 1 - core)):
        tokens = ref[0, :tok, :]
        meta = ref[0, tok:, :tok].astype(F32)
        g0, g1, i0, i1 = (meta[k : k + 1, :] for k in range(4))
        hit0, hit1 = (i0 == me), (i1 == me)
        named = jnp.where(hit0, 1.0, jnp.where(hit1, 1.0, 0.0))
        picked = jnp.where(hit0, g0, jnp.where(hit1, g1, 0.0))
        rank = lax.dot_general(
            jnp.broadcast_to(named, (8, tok)).astype(BF),
            tri,
            (((1,), (0,)), ((), ())),
            preferred_element_type=F32,
        )[0:1]
        rank = jnp.where(named > 0.0, rank, -1.0).astype(jnp.int32)
        onehot = jnp.where(place == rank, 1.0, 0.0)
        rows = lax.dot_general(
            onehot.astype(BF), tokens, (((1,), (0,)), ((), ())), preferred_element_type=F32
        )
        weight = jnp.sum(onehot * picked, axis=1, keepdims=True)
        grp[pl.ds(pl.multiple_of(at * tok, tok), tok), :] = tokens
        slot = pl.ds(pl.multiple_of(at * cap, cap), cap)
        recv[slot, :] = rows.astype(BF)
        scal[slot, :] = (weight * rows).astype(BF)
        gate[slot, :] = weight


def dispatch(scalars, mine, partner, tok, slots):
    width = mine.shape[2]
    cap2 = slots // NY
    taken = pl.BlockSpec((1, *mine.shape[1:]), lambda k: (k, 0, 0))

    def given(rows, cols):
        return pl.BlockSpec((rows, cols), lambda k: (k, 0))

    return pl.pallas_call(
        dispatch_kernel,
        name="dispatch",
        grid=(NY,),
        out_shape=(
            jax.ShapeDtypeStruct((NY * NC * tok, width), BF),
            jax.ShapeDtypeStruct((slots, width), BF),
            jax.ShapeDtypeStruct((slots, width), BF),
            jax.ShapeDtypeStruct((slots, 1), F32),
        ),
        in_specs=[pl.BlockSpec(memory_space=pltpu.SMEM), taken, taken],
        out_specs=(given(NC * tok, width), given(cap2, width), given(cap2, width), given(cap2, 1)),
        compiler_params=pltpu.CompilerParams(vmem_limit_bytes=24 << 20),
        cost_estimate=pl.CostEstimate(flops=200_000_000, bytes_accessed=10_000_000, transcendentals=0),
    )(scalars, mine, partner)


def terms_kernel(hidden, scal, tsh, ta, tb):
    out = lax.dot_general(
        hidden[...], scal[...], (((0,), (0,)), ((), ())), preferred_element_type=F32
    )
    nx, half = tb.shape[1], tb.shape[3]
    rows = hidden.shape[1] // nx
    out = out.astype(BF).reshape(nx, rows, half)

    @pl.when(pl.program_id(0) == 0)
    def _():
        ta[:, 0, :rows, :] = out
        ta[:, 0, rows:, :] = tsh[0]

    @pl.when(pl.program_id(0) == 1)
    def _():
        tb[0, :, :rows, :] = out
        tb[0, :, rows:, :] = tsh[0]


def terms(hidden, scal, tsh):
    slots, hid = hidden.shape
    half = scal.shape[1] // 2
    rows, extra = hid // (NZ * NX), tsh.shape[2]
    tail = (rows + extra, half)
    return pl.pallas_call(
        terms_kernel,
        name="terms",
        grid=(2, NZ),
        out_shape=(
            jax.ShapeDtypeStruct((NX, NZ, *tail), BF),
            jax.ShapeDtypeStruct((NZ, NX, *tail), BF),
        ),
        in_specs=[
            pl.BlockSpec((slots, hid // NZ), lambda j, k: (0, k)),
            pl.BlockSpec((slots, half), lambda j, k: (0, j)),
            pl.BlockSpec((1, NX, extra, half), lambda j, k: (k, 0, 0, j)),
        ],
        out_specs=(
            pl.BlockSpec((NX, 1, *tail), lambda j, k: (0, k * (1 - j) + (NZ - 1) * j, 0, 0)),
            pl.BlockSpec((1, NX, *tail), lambda j, k: (k * j, 0, 0, 0)),
        ),
        compiler_params=pltpu.CompilerParams(vmem_limit_bytes=24 << 20),
        cost_estimate=pl.CostEstimate(
            flops=4 * slots * hid * half, bytes_accessed=20_000_000, transcendentals=0
        ),
    )(hidden, scal, tsh)


RAW_STEPS = 3
OFFLOADED = 1152
GROUPS = ((0, 1, 7), (2, 6), (3, 5), (4,))


def raw_kernel(parts, sc, rows, gate, pre, a_ref, *refs):
    *b_refs, _, _, out, wsh, score, whole, small = refs
    n_rows = whole.shape[0] // NX
    extra = small.shape[0] // NX
    half = a_ref.shape[3]

    @pl.when(pl.program_id(1) == 0)
    def _():
        for k in range(NX):
            whole[k * n_rows : (k + 1) * n_rows, :half] = a_ref[0, k, :n_rows, :]
            small[k * extra : (k + 1) * extra, :half] = a_ref[0, k, n_rows:, :].astype(F32)
        at = 0
        for p, n in enumerate(parts):
            mine = b_refs[at : at + n]
            at += n

            @pl.when(pl.program_id(0) == p)
            def _():
                for k in range(NX):
                    b_ref, i = mine[k * n // NX], k % (NX // n)
                    whole[k * n_rows : (k + 1) * n_rows, half:] = b_ref[i, :n_rows, :]
                    small[k * extra : (k + 1) * extra, half:] = b_ref[i, n_rows:, :].astype(F32)

        wsh[...] = small[...].astype(BF)

    raw = lax.dot_general(
        rows[...], whole[...], (((1,), (1,)), ((), ())), preferred_element_type=F32
    )
    value, slope = gelu_pair(pre[...].astype(F32))
    out[...] = (gate[...] * raw * slope).astype(BF)
    score[0] = jnp.sum(value * raw, axis=1, keepdims=True)


def raw_blocks(scalars, rows, gate, pre, a_whole, b_group, carried):
    slots, width = rows.shape
    hid = pre.shape[1]
    block, step = hid // NZ, slots // RAW_STEPS
    n_rows = block // NX
    extra = a_whole.shape[2] - n_rows
    b_group = [list(b) if isinstance(b, tuple) else [b] for b in b_group]
    parts = tuple(len(b) for b in b_group)
    b_list = sum(b_group, [])
    in_specs = [
        pl.BlockSpec((step, width), lambda p, i, sc: (i, 0)),
        pl.BlockSpec((step, 1), lambda p, i, sc: (i, 0)),
        pl.BlockSpec((step, block), lambda p, i, sc: (i, sc[p])),
        pl.BlockSpec((1, *a_whole.shape[1:]), lambda p, i, sc: (sc[p], 0, 0, 0)),
    ]
    in_specs += [pl.BlockSpec(b.shape, lambda p, i, sc: (0, 0, 0)) for b in b_list]
    args = [rows, gate, pre, a_whole, *b_list]
    aliases = {}
    in_specs += [pl.BlockSpec(memory_space=pl.ANY)] * 2
    if carried is not None:
        aliases = {1 + len(args): 0, 2 + len(args): 1}
        args += list(carried)
    else:
        args += [gate, gate]
    n = len(parts)
    return pl.pallas_call(
        functools.partial(raw_kernel, parts),
        name="raw",
        out_shape=(
            jax.ShapeDtypeStruct((slots, hid), BF),
            jax.ShapeDtypeStruct((NZ * NX * extra, width), BF),
            jax.ShapeDtypeStruct((n, slots, 1), F32),
        ),
        grid_spec=pltpu.PrefetchScalarGridSpec(
            num_scalar_prefetch=1,
            grid=(n, RAW_STEPS),
            in_specs=in_specs,
            out_specs=(
                pl.BlockSpec((step, block), lambda p, i, sc: (i, sc[p])),
                pl.BlockSpec((NX * extra, width), lambda p, i, sc: (sc[p], 0)),
                pl.BlockSpec((1, step, 1), lambda p, i, sc: (p, i, 0)),
            ),
            scratch_shapes=[pltpu.VMEM((block, width), BF), pltpu.VMEM((NX * extra, width), F32)],
        ),
        input_output_aliases=aliases,
        compiler_params=pltpu.CompilerParams(vmem_limit_bytes=16 << 20),
        cost_estimate=pl.CostEstimate(
            flops=2 * n * slots * block * width,
            bytes_accessed=5_000_000 * n,
            transcendentals=n * slots * block,
        ),
    )(scalars, *args)


def to_all(a, axis, n):
    many = jnp.broadcast_to(a[None], (n, *a.shape))
    return lax.all_to_all(many, axis, 0, 0, tiled=True)


def body(grad_out, expert_ids, gates, routed_pre, routed_down, shared_pre, shared_down):
    z, x, y, c = (lax.axis_index(a) for a in ("z", "x", "y", "c"))
    owner = y * NC + c
    n_exp = NY * NC
    tok, width = grad_out.shape
    slots = routed_pre.shape[2]
    cap = slots // n_exp

    shard = jnp.concatenate([routed_down[0], shared_down], axis=0)
    a_whole = lax.all_gather(shard[:, :OFFLOADED], DP)
    a_whole = a_whole.reshape(NZ, NX, *a_whole.shape[1:])
    b_shard = shard[:, OFFLOADED:]
    around = [b_shard] + [hop(b_shard, "x", -k) for k in range(1, NX)]
    b_all = lax.dynamic_slice_in_dim(jnp.stack(around + around[:-1]), (NX - x) % NX, NX, 0)
    b_pieces = gather_eight(b_all, "z", cut_rows)

    metas = jnp.concatenate([gates.astype(BF).T, expert_ids.astype(BF).T], axis=0)
    metas = jnp.pad(metas, ((0, 8 - metas.shape[0]), (0, width - tok)))
    mine = to_all(jnp.concatenate([grad_out, metas], axis=0), "y", NY)
    partner = hop(mine, "c", 1)

    pre = routed_pre[0, 0]
    hidden_b = gelu_pair(pre.astype(F32))[0].astype(BF)
    shared_b = gelu_pair(shared_pre.astype(F32))[0].astype(BF)

    scalars = jnp.stack([owner, c]).astype(jnp.int32)
    group_rows, recv_rows, scaled, gate_col = dispatch(scalars, mine, partner, tok, slots)

    shared_term = lax.dot_general(
        shared_b, group_rows, (((0,), (0,)), ((), ())), preferred_element_type=F32
    ).astype(BF)
    ta, tb = terms(hidden_b, scaled, shared_term.reshape(NZ, NX, -1, width))

    def along(t, place, n):
        return lambda r: lax.dynamic_index_in_dim(t, (place + r) % n, 0, keepdims=False)

    sum_a = sum_ring(along(ta, x, NX), NX, "x", cut_rows, join_rows).astype(BF)
    sum_b = sum_ring(along(tb, z, NZ), NZ, "z", cut_rows, join_rows).astype(BF)
    sum_a = lax.all_to_all(sum_a, "z", 0, 0, tiled=True)
    sum_b = lax.all_to_all(sum_b, "x", 0, 0, tiled=True)
    sum_a = sum_a.astype(F32).sum(axis=0)
    sum_b = sum_b.astype(F32).sum(axis=0)
    total = jnp.concatenate([sum_a, sum_b], axis=1)
    rows = routed_down.shape[1]

    carried, scores = None, []
    for group in GROUPS:
        sc = jnp.stack([(z + (NZ - j)) % NZ for j in group]).astype(jnp.int32)
        pieces = [b_pieces[j] for j in group]
        out, wsh, score = raw_blocks(sc, recv_rows, gate_col, pre, a_whole, pieces, carried)
        carried = (out, wsh)
        scores.append(score)
    routed_pre_grad, whole_shared = carried
    slot_score = jnp.concatenate(scores, axis=0).sum(axis=0)
    returned = lax.all_to_all(slot_score.reshape(n_exp, cap), EXPERT, 0, 0, tiled=True)

    labels = jnp.arange(n_exp, dtype=jnp.int32)
    onehot = expert_ids[:, :, None] == labels[None, None, :]
    named = jnp.any(onehot, axis=1).astype(F32)
    order = jnp.arange(tok, dtype=jnp.int32)
    tri = (order[None, :] < order[:, None]).astype(F32)
    counts = lax.dot_general(tri, named, (((1,), (0,)), ((), ())), preferred_element_type=F32)
    rank = jnp.sum(jnp.where(onehot, counts[:, None, :], 0.0), axis=2).astype(jnp.int32)
    slot = expert_ids * cap + rank
    each = jnp.arange(slots, dtype=jnp.int32)
    gate_grad = jnp.sum(
        jnp.where(slot[:, :, None] == each[None, None, :], returned.reshape(1, 1, slots), 0.0), axis=2
    )

    raw_shared = lax.dot_general(
        group_rows, whole_shared, (((1,), (1,)), ((), ())), preferred_element_type=F32
    )
    shared_pre_grad = (raw_shared * gelu_pair(shared_pre.astype(F32))[1]).astype(BF)
    return (
        routed_pre_grad.reshape(routed_pre.shape),
        total[:rows].reshape(1, rows, width),
        shared_pre_grad,
        total[rows:],
        gate_grad,
    )


def solution(mesh):
    split = Mesh(mesh.devices.reshape(NZ, NX, NY, NC), ("z", "x", "y", "c"))
    placed = (
        P(DP_EXPERT, None),
        P(DP_EXPERT, None),
        P(DP_EXPERT, None),
        P(DP, EXPERT, None, None),
        P(EXPERT, DP, None),
        P(DP, EXPERT),
        P(EXPERT_DP, None),
    )
    return jax.shard_map(
        body,
        mesh=split,
        in_specs=placed,
        out_specs=(
            P(DP, EXPERT, None, None),
            P(EXPERT, DP, None),
            P(DP, EXPERT),
            P(EXPERT_DP, None),
            P(DP_EXPERT, None),
        ),
        check_vma=False,
    )
```

```python
import functools

import jax
import jax.numpy as jnp
from jax import lax
from jax.experimental import pallas as pl
from jax.experimental.pallas import tpu as pltpu
from jax.sharding import Mesh
from jax.sharding import PartitionSpec as P


DP = ("z", "x")
EXPERT = ("y", "c")
DP_EXPERT = ("z", "x", "y", "c")
EXPERT_DP = ("y", "c", "z", "x")
NZ, NX, NY, NC = 8, 4, 4, 2


SQRT_TWO_PI = 0.7978845608028654
BF = jnp.bfloat16
F32 = jnp.float32


def hop(a, axis, by):
    n = lax.axis_size(axis)
    return lax.ppermute(a, axis, [(i, (i + by) % n) for i in range(n)])


def gelu_pair(inputs):
    cubic = inputs * inputs * inputs
    tangent = jnp.tanh(SQRT_TWO_PI * (inputs + 0.044715 * cubic))
    value = 0.5 * inputs * (1.0 + tangent)
    slope = 0.5 * (1.0 + tangent) + 0.5 * inputs * (1.0 - tangent * tangent) * SQRT_TWO_PI * (
        1.0 + 3.0 * 0.044715 * inputs * inputs
    )
    return (value, slope)


def added(a, b):
    return (a.astype(F32) + b.astype(F32)).astype(BF)


def gather_eight(a, axis, cut):
    right = [a]
    left = [a]
    for _ in range(1, 4):
        right.append(hop(right[-1], axis, 1))
        left.append(hop(left[-1], axis, -1))
    far = (hop(cut(right[3])[0], axis, 1), hop(cut(left[3])[1], axis, -1))
    return right[0], right[1], right[2], right[3], far, left[3], left[2], left[1]


def cut_rows(a):
    half = a.shape[0] // 2
    return a[:half], a[half:]


def sum_ring(block, n, axis):
    far = block(n // 2)
    half = far.shape[0] // 2
    right = hop(far[:half], axis, 1)
    left = hop(far[half:], axis, -1)
    rest = ((0, 0),) * (far.ndim - 1)
    for k, r in enumerate(range(n // 2 - 1, 0, -1)):
        right, left = lax.optimization_barrier((right, left))
        if k == 0:
            right = jnp.pad(right, ((0, half), *rest))
            left = jnp.pad(left, ((half, 0), *rest))
        right = hop(added(block(r), right), axis, 1)
        left = hop(added(block(n - r), left), axis, -1)
    right, left = lax.optimization_barrier((right, left))
    return block(0).astype(F32) + right.astype(F32) + left.astype(F32)


def dispatch_kernel(sc, mine, partner, grp, recv, scal, gate):
    owner, core = sc[0], sc[1]
    tok, cap = grp.shape[0] // 2, recv.shape[0] // 2
    me = owner.astype(F32)
    earlier = lax.broadcasted_iota(jnp.int32, (tok, tok), 0)
    later = lax.broadcasted_iota(jnp.int32, (tok, tok), 1)
    tri = jnp.where(earlier < later, 1.0, 0.0).astype(BF)
    place = lax.broadcasted_iota(jnp.int32, (cap, tok), 0)
    for ref, at in ((mine, core), (partner, 1 - core)):
        tokens = ref[0, :tok, :]
        meta = ref[0, tok:, :tok].astype(F32)
        g0, g1, i0, i1 = (meta[k : k + 1, :] for k in range(4))
        hit0, hit1 = (i0 == me), (i1 == me)
        named = jnp.where(hit0, 1.0, jnp.where(hit1, 1.0, 0.0))
        picked = jnp.where(hit0, g0, jnp.where(hit1, g1, 0.0))
        rank = lax.dot_general(
            jnp.broadcast_to(named, (8, tok)).astype(BF),
            tri,
            (((1,), (0,)), ((), ())),
            preferred_element_type=F32,
        )[0:1]
        rank = jnp.where(named > 0.0, rank, -1.0).astype(jnp.int32)
        onehot = jnp.where(place == rank, 1.0, 0.0)
        rows = lax.dot_general(
            onehot.astype(BF), tokens, (((1,), (0,)), ((), ())), preferred_element_type=F32
        )
        weight = jnp.sum(onehot * picked, axis=1, keepdims=True)
        grp[pl.ds(pl.multiple_of(at * tok, tok), tok), :] = tokens
        slot = pl.ds(pl.multiple_of(at * cap, cap), cap)
        recv[slot, :] = rows.astype(BF)
        scal[slot, :] = (weight * rows).astype(BF)
        gate[slot, :] = weight


def dispatch(scalars, mine, partner, tok, slots):
    width = mine.shape[2]
    cap2 = slots // NY
    taken = pl.BlockSpec((1, *mine.shape[1:]), lambda k: (k, 0, 0))

    def given(rows, cols):
        return pl.BlockSpec((rows, cols), lambda k: (k, 0))

    return pl.pallas_call(
        dispatch_kernel,
        name="dispatch",
        grid=(NY,),
        out_shape=(
            jax.ShapeDtypeStruct((NY * NC * tok, width), BF),
            jax.ShapeDtypeStruct((slots, width), BF),
            jax.ShapeDtypeStruct((slots, width), BF),
            jax.ShapeDtypeStruct((slots, 1), F32),
        ),
        in_specs=[pl.BlockSpec(memory_space=pltpu.SMEM), taken, taken],
        out_specs=(given(NC * tok, width), given(cap2, width), given(cap2, width), given(cap2, 1)),
        compiler_params=pltpu.CompilerParams(vmem_limit_bytes=24 << 20),
        cost_estimate=pl.CostEstimate(flops=200_000_000, bytes_accessed=10_000_000, transcendentals=0),
    )(scalars, mine, partner)


def terms_kernel(hidden, scal, tsh, ta, tb):
    out = lax.dot_general(
        hidden[...], scal[...], (((0,), (0,)), ((), ())), preferred_element_type=F32
    )
    nx, part = tb.shape[1], tb.shape[3]
    rows = hidden.shape[1] // nx
    out = out.astype(BF).reshape(nx, rows, part)

    @pl.when(pl.program_id(0) == 0)
    def _():
        ta[:, 0, :rows, :] = out
        ta[:, 0, rows:, :] = tsh[0]

    @pl.when(pl.program_id(0) > 0)
    def _():
        tb[0, :, :rows, :] = out
        tb[0, :, rows:, :] = tsh[0]


def terms(hidden, scal, tsh):
    slots, hid = hidden.shape
    width = scal.shape[1]
    part = SUMS_OFFLOADED
    rows, extra = hid // (NZ * NX), tsh.shape[2]
    high = rows + extra
    return pl.pallas_call(
        terms_kernel,
        name="terms",
        grid=(width // part, NZ),
        out_shape=(
            jax.ShapeDtypeStruct((NX, NZ, high, part), BF),
            jax.ShapeDtypeStruct((NZ, NX, high, width - part), BF),
        ),
        in_specs=[
            pl.BlockSpec((slots, hid // NZ), lambda j, k: (0, k)),
            pl.BlockSpec((slots, part), lambda j, k: (0, j)),
            pl.BlockSpec((1, NX, extra, part), lambda j, k: (k, 0, 0, j)),
        ],
        out_specs=(
            pl.BlockSpec(
                (NX, 1, high, part), lambda j, k: (0, jnp.where(j == 0, k, NZ - 1), 0, 0)
            ),
            pl.BlockSpec(
                (1, NX, high, part),
                lambda j, k: (jnp.where(j == 0, 0, k), 0, 0, jnp.maximum(j - 1, 0)),
            ),
        ),
        compiler_params=pltpu.CompilerParams(vmem_limit_bytes=24 << 20),
        cost_estimate=pl.CostEstimate(
            flops=2 * slots * hid * width, bytes_accessed=20_000_000, transcendentals=0
        ),
    )(hidden, scal, tsh)


RAW_STEPS = 3
GATHER_OFFLOADED = 896
SUMS_OFFLOADED = 512


def raw_kernel(parts, sc, rows, gate, pre, a_ref, *refs):
    *b_refs, out, wsh, score, whole, small = refs
    n_rows = whole.shape[0] // NX
    extra = small.shape[0] // NX
    half = a_ref.shape[3]

    @pl.when(pl.program_id(1) == 0)
    def _():
        for k in range(NX):
            whole[k * n_rows : (k + 1) * n_rows, :half] = a_ref[0, k, :n_rows, :]
            small[k * extra : (k + 1) * extra, :half] = a_ref[0, k, n_rows:, :].astype(F32)
        at = 0
        for p, n in enumerate(parts):
            mine = b_refs[at : at + n]
            at += n

            @pl.when(pl.program_id(0) == p)
            def _():
                for k in range(NX):
                    b_ref, i = mine[k * n // NX], k % (NX // n)
                    whole[k * n_rows : (k + 1) * n_rows, half:] = b_ref[i, :n_rows, :]
                    small[k * extra : (k + 1) * extra, half:] = b_ref[i, n_rows:, :].astype(F32)

        wsh[...] = small[...].astype(BF)

    raw = lax.dot_general(
        rows[...], whole[...], (((1,), (1,)), ((), ())), preferred_element_type=F32
    )
    value, slope = gelu_pair(pre[...].astype(F32))
    out[...] = (gate[...] * raw * slope).astype(BF)
    score[0] = jnp.sum(value * raw, axis=1, keepdims=True)


def raw_blocks(scalars, rows, gate, pre, a_whole, b_group):
    slots, width = rows.shape
    hid = pre.shape[1]
    block, step = hid // NZ, slots // RAW_STEPS
    n_rows = block // NX
    extra = a_whole.shape[2] - n_rows
    b_group = [list(b) if isinstance(b, tuple) else [b] for b in b_group]
    parts = tuple(len(b) for b in b_group)
    b_list = sum(b_group, [])
    in_specs = [
        pl.BlockSpec((step, width), lambda p, i, sc: (i, 0)),
        pl.BlockSpec((step, 1), lambda p, i, sc: (i, 0)),
        pl.BlockSpec((step, block), lambda p, i, sc: (i, sc[p])),
        pl.BlockSpec((1, *a_whole.shape[1:]), lambda p, i, sc: (sc[p], 0, 0, 0)),
    ]
    once = pl.Buffered(1)
    in_specs += [pl.BlockSpec(b.shape, lambda p, i, sc: (0, 0, 0), pipeline_mode=once) for b in b_list]
    return pl.pallas_call(
        functools.partial(raw_kernel, parts),
        name="raw",
        out_shape=(
            jax.ShapeDtypeStruct((slots, hid), BF),
            jax.ShapeDtypeStruct((NZ * NX * extra, width), BF),
            jax.ShapeDtypeStruct((NZ, slots, 1), F32),
        ),
        grid_spec=pltpu.PrefetchScalarGridSpec(
            num_scalar_prefetch=1,
            grid=(NZ, RAW_STEPS),
            in_specs=in_specs,
            out_specs=(
                pl.BlockSpec((step, block), lambda p, i, sc: (i, sc[p])),
                pl.BlockSpec((NX * extra, width), lambda p, i, sc: (sc[p], 0)),
                pl.BlockSpec((1, step, 1), lambda p, i, sc: (p, i, 0)),
            ),
            scratch_shapes=[pltpu.VMEM((block, width), BF), pltpu.VMEM((NX * extra, width), F32)],
        ),
        compiler_params=pltpu.CompilerParams(vmem_limit_bytes=24 << 20),
        cost_estimate=pl.CostEstimate(
            flops=2 * slots * hid * width, bytes_accessed=22_000_000, transcendentals=slots * hid
        ),
    )(scalars, rows, gate, pre, a_whole, *b_list)


def to_all(a, axis, n):
    many = jnp.broadcast_to(a[None], (n, *a.shape))
    return lax.all_to_all(many, axis, 0, 0, tiled=True)


def body(grad_out, expert_ids, gates, routed_pre, routed_down, shared_pre, shared_down):
    z, x, y, c = (lax.axis_index(a) for a in ("z", "x", "y", "c"))
    owner = y * NC + c
    n_exp = NY * NC
    tok, width = grad_out.shape
    slots = routed_pre.shape[2]
    cap = slots // n_exp

    shard = jnp.concatenate([routed_down[0], shared_down], axis=0)
    a_whole = lax.all_gather(shard[:, :GATHER_OFFLOADED], DP)
    a_whole = a_whole.reshape(NZ, NX, *a_whole.shape[1:])
    b_shard = shard[:, GATHER_OFFLOADED:]
    around = [b_shard] + [hop(b_shard, "x", -k) for k in range(1, NX)]
    b_all = lax.dynamic_slice_in_dim(jnp.stack(around + around[:-1]), (NX - x) % NX, NX, 0)
    b_pieces = gather_eight(b_all, "z", cut_rows)

    metas = jnp.concatenate([gates.astype(BF).T, expert_ids.astype(BF).T], axis=0)
    metas = jnp.pad(metas, ((0, 8 - metas.shape[0]), (0, width - tok)))
    mine = to_all(jnp.concatenate([grad_out, metas], axis=0), "y", NY)
    partner = hop(mine, "c", 1)

    pre = routed_pre[0, 0]
    hidden_b = gelu_pair(pre.astype(F32))[0].astype(BF)
    shared_b = gelu_pair(shared_pre.astype(F32))[0].astype(BF)

    scalars = jnp.stack([owner, c]).astype(jnp.int32)
    group_rows, recv_rows, scaled, gate_col = dispatch(scalars, mine, partner, tok, slots)

    shared_term = lax.dot_general(
        shared_b, group_rows, (((0,), (0,)), ((), ())), preferred_element_type=F32
    ).astype(BF)
    ta, tb = terms(hidden_b, scaled, shared_term.reshape(NZ, NX, -1, width))

    sum_a = lax.psum_scatter(
        ta.reshape(-1, ta.shape[3]), "x", scatter_dimension=0, tiled=True
    )
    sum_a = lax.psum_scatter(sum_a, "z", scatter_dimension=0, tiled=True)

    def along(r):
        return lax.dynamic_index_in_dim(tb, (z + r) % NZ, 0, keepdims=False)

    sum_b = sum_ring(along, NZ, "z").astype(BF)
    sum_b = lax.all_to_all(sum_b, "x", 0, 0, tiled=True)
    sum_a = sum_a.astype(F32)
    sum_b = sum_b.astype(F32).sum(axis=0)
    total = jnp.concatenate([sum_a, sum_b], axis=1)
    rows = routed_down.shape[1]

    sc = jnp.stack([(z + (NZ - j)) % NZ for j in range(NZ)]).astype(jnp.int32)
    routed_pre_grad, whole_shared, score = raw_blocks(
        sc, recv_rows, gate_col, pre, a_whole, b_pieces
    )
    slot_score = score.sum(axis=0)
    returned = lax.all_to_all(slot_score.reshape(n_exp, cap), EXPERT, 0, 0, tiled=True)

    labels = jnp.arange(n_exp, dtype=jnp.int32)
    onehot = expert_ids[:, :, None] == labels[None, None, :]
    named = jnp.any(onehot, axis=1).astype(F32)
    order = jnp.arange(tok, dtype=jnp.int32)
    tri = (order[None, :] < order[:, None]).astype(F32)
    counts = lax.dot_general(tri, named, (((1,), (0,)), ((), ())), preferred_element_type=F32)
    rank = jnp.sum(jnp.where(onehot, counts[:, None, :], 0.0), axis=2).astype(jnp.int32)
    slot = expert_ids * cap + rank
    each = jnp.arange(slots, dtype=jnp.int32)
    gate_grad = jnp.sum(
        jnp.where(slot[:, :, None] == each[None, None, :], returned.reshape(1, 1, slots), 0.0), axis=2
    )

    raw_shared = lax.dot_general(
        group_rows, whole_shared, (((1,), (1,)), ((), ())), preferred_element_type=F32
    )
    shared_pre_grad = (raw_shared * gelu_pair(shared_pre.astype(F32))[1]).astype(BF)
    return (
        routed_pre_grad.reshape(routed_pre.shape),
        total[:rows].reshape(1, rows, width),
        shared_pre_grad,
        total[rows:],
        gate_grad,
    )


def solution(mesh):
    split = Mesh(mesh.devices.reshape(NZ, NX, NY, NC), ("z", "x", "y", "c"))
    placed = (
        P(DP_EXPERT, None),
        P(DP_EXPERT, None),
        P(DP_EXPERT, None),
        P(DP, EXPERT, None, None),
        P(EXPERT, DP, None),
        P(DP, EXPERT),
        P(EXPERT_DP, None),
    )
    return jax.shard_map(
        body,
        mesh=split,
        in_specs=placed,
        out_specs=(
            P(DP, EXPERT, None, None),
            P(EXPERT, DP, None),
            P(DP, EXPERT),
            P(EXPERT_DP, None),
            P(DP_EXPERT, None),
        ),
        check_vma=False,
    )
```

```python
import jax
import jax.numpy as jnp
from jax import lax
from jax.experimental import pallas as pl
from jax.experimental.pallas import tpu as pltpu
from jax.sharding import Mesh
from jax.sharding import PartitionSpec as P


DP = ("z", "x")
EXPERT = ("y", "c")
DP_EXPERT = ("z", "x", "y", "c")
EXPERT_DP = ("y", "c", "z", "x")
NZ, NX, NY, NC = 8, 4, 4, 2


SQRT_TWO_PI = 0.7978845608028654
BF = jnp.bfloat16
F32 = jnp.float32


def hop(a, axis, by):
    n = lax.axis_size(axis)
    return lax.ppermute(a, axis, [(i, (i + by) % n) for i in range(n)])


def gelu_pair(inputs):
    cubic = inputs * inputs * inputs
    tangent = jnp.tanh(SQRT_TWO_PI * (inputs + 0.044715 * cubic))
    value = 0.5 * inputs * (1.0 + tangent)
    slope = 0.5 * (1.0 + tangent) + 0.5 * inputs * (1.0 - tangent * tangent) * SQRT_TWO_PI * (
        1.0 + 3.0 * 0.044715 * inputs * inputs
    )
    return (value, slope)


def added(a, b):
    return (a.astype(F32) + b.astype(F32)).astype(BF)


def ring_gather(a, axis, dim):
    n = lax.axis_size(axis)
    half = a.shape[dim] // 2
    right, left = [a], [a]
    for _ in range(1, n // 2):
        right.append(hop(right[-1], axis, 1))
        left.append(hop(left[-1], axis, -1))
    first = lax.slice_in_dim(right[-1], 0, half, axis=dim)
    second = lax.slice_in_dim(left[-1], half, 2 * half, axis=dim)
    far = (hop(first, axis, 1), hop(second, axis, -1))
    return right, far, left[:0:-1]


def sum_ring(block, n, axis, dim):
    far = block(n // 2)
    half = far.shape[dim] // 2
    first = lax.slice_in_dim(far, 0, half, axis=dim)
    second = lax.slice_in_dim(far, half, 2 * half, axis=dim)
    right = hop(first, axis, 1)
    left = hop(second, axis, -1)
    for k, r in enumerate(range(n // 2 - 1, 0, -1)):
        right, left = lax.optimization_barrier((right, left))
        if k == 0:
            grown = [(0, 0)] * far.ndim
            grown[dim] = (0, half)
            right = jnp.pad(right, grown)
            grown[dim] = (half, 0)
            left = jnp.pad(left, grown)
        right = hop(added(block(r), right), axis, 1)
        left = hop(added(block(n - r), left), axis, -1)
    right, left = lax.optimization_barrier((right, left))
    return block(0).astype(F32) + right.astype(F32) + left.astype(F32)


def dispatch_kernel(sc, mine, partner, grp, recv, scal, gate):
    owner, core = sc[0], sc[1]
    tok, cap = grp.shape[0] // 2, recv.shape[0] // 2
    me = owner.astype(F32)
    earlier = lax.broadcasted_iota(jnp.int32, (tok, tok), 0)
    later = lax.broadcasted_iota(jnp.int32, (tok, tok), 1)
    tri = jnp.where(earlier < later, 1.0, 0.0).astype(BF)
    place = lax.broadcasted_iota(jnp.int32, (cap, tok), 0)
    for ref, at in ((mine, core), (partner, 1 - core)):
        tokens = ref[0, :tok, :]
        meta = ref[0, tok:, :tok].astype(F32)
        g0, g1, i0, i1 = (meta[k : k + 1, :] for k in range(4))
        hit0, hit1 = (i0 == me), (i1 == me)
        named = jnp.where(hit0, 1.0, jnp.where(hit1, 1.0, 0.0))
        picked = jnp.where(hit0, g0, jnp.where(hit1, g1, 0.0))
        rank = lax.dot_general(
            jnp.broadcast_to(named, (8, tok)).astype(BF),
            tri,
            (((1,), (0,)), ((), ())),
            preferred_element_type=F32,
        )[0:1]
        rank = jnp.where(named > 0.0, rank, -1.0).astype(jnp.int32)
        onehot = jnp.where(place == rank, 1.0, 0.0)
        rows = lax.dot_general(
            onehot.astype(BF), tokens, (((1,), (0,)), ((), ())), preferred_element_type=F32
        )
        weight = jnp.sum(onehot * picked, axis=1, keepdims=True)
        grp[pl.ds(pl.multiple_of(at * tok, tok), tok), :] = tokens
        slot = pl.ds(pl.multiple_of(at * cap, cap), cap)
        recv[slot, :] = rows.astype(BF)
        scal[slot, :] = (weight * rows).astype(BF)
        gate[slot, :] = weight


def dispatch(scalars, mine, partner, tok, slots):
    width = mine.shape[2]
    cap2 = slots // NY
    taken = pl.BlockSpec((1, *mine.shape[1:]), lambda k: (k, 0, 0))

    def given(rows, cols):
        return pl.BlockSpec((rows, cols), lambda k: (k, 0))

    return pl.pallas_call(
        dispatch_kernel,
        name="dispatch",
        grid=(NY,),
        out_shape=(
            jax.ShapeDtypeStruct((NY * NC * tok, width), BF),
            jax.ShapeDtypeStruct((slots, width), BF),
            jax.ShapeDtypeStruct((slots, width), BF),
            jax.ShapeDtypeStruct((slots, 1), F32),
        ),
        in_specs=[pl.BlockSpec(memory_space=pltpu.SMEM), taken, taken],
        out_specs=(given(NC * tok, width), given(cap2, width), given(cap2, width), given(cap2, 1)),
        compiler_params=pltpu.CompilerParams(vmem_limit_bytes=24 << 20),
        cost_estimate=pl.CostEstimate(flops=200_000_000, bytes_accessed=10_000_000, transcendentals=0),
    )(scalars, mine, partner)


def terms_kernel(hidden, scal, tsh, ta, tb):
    out = lax.dot_general(
        hidden[...], scal[...], (((0,), (0,)), ((), ())), preferred_element_type=F32
    )
    nx, half = ta.shape[1], ta.shape[3]
    rows = hidden.shape[1] // nx
    out = out.astype(BF).reshape(nx, rows, 2 * half)
    ta[0, :, :rows, :] = out[:, :, :half]
    tb[:, 0, :rows, :] = out[:, :, half:]
    ta[0, :, rows:, :] = tsh[0, :, :, :half]
    tb[:, 0, rows:, :] = tsh[0, :, :, half:]


def terms(hidden, scal, tsh):
    slots, hid = hidden.shape
    width = scal.shape[1]
    rows, extra = hid // (NZ * NX), tsh.shape[2]
    tail = (rows + extra, width // 2)
    return pl.pallas_call(
        terms_kernel,
        name="terms",
        grid=(NZ,),
        out_shape=(
            jax.ShapeDtypeStruct((NZ, NX, *tail), BF),
            jax.ShapeDtypeStruct((NX, NZ, *tail), BF),
        ),
        in_specs=[
            pl.BlockSpec((slots, hid // NZ), lambda k: (0, k)),
            pl.BlockSpec((slots, width), lambda k: (0, 0)),
            pl.BlockSpec((1, NX, extra, width), lambda k: (k, 0, 0, 0)),
        ],
        out_specs=(
            pl.BlockSpec((1, NX, *tail), lambda k: (k, 0, 0, 0)),
            pl.BlockSpec((NX, 1, *tail), lambda k: (0, k, 0, 0)),
        ),
        compiler_params=pltpu.CompilerParams(vmem_limit_bytes=24 << 20),
        cost_estimate=pl.CostEstimate(
            flops=2 * slots * hid * width, bytes_accessed=20_000_000, transcendentals=0
        ),
    )(hidden, scal, tsh)


RAW_STEPS = 3


def raw_kernel(sc, rows, gate, pre, a_ref, own, right, far0, far1, left, out, wsh, score, whole, small):
    n_rows = whole.shape[0] // NX
    extra = small.shape[0] // NX
    half = a_ref.shape[3]
    x = sc[NZ]

    def put(ref, r):
        source = (x + (NX - r)) % NX
        at = pl.ds(pl.multiple_of(source * n_rows, n_rows), n_rows)
        whole[at, half:] = ref[0, :n_rows, :]
        at = pl.ds(pl.multiple_of(source * extra, extra), extra)
        small[at, half:] = ref[0, n_rows:, :].astype(F32)

    @pl.when(pl.program_id(1) == 0)
    def _():
        for k in range(NX):
            whole[k * n_rows : (k + 1) * n_rows, :half] = a_ref[0, k, :n_rows, :]
            small[k * extra : (k + 1) * extra, :half] = a_ref[0, k, n_rows:, :].astype(F32)
        put(own, 0)
        put(right, 1)
        put(left, 3)

        @pl.when(pl.program_id(0) < NZ // 2)
        def _():
            put(far0, 2)

        @pl.when(pl.program_id(0) >= NZ // 2)
        def _():
            put(far1, 2)

        wsh[...] = small[...].astype(BF)

    raw = lax.dot_general(
        rows[...], whole[...], (((1,), (1,)), ((), ())), preferred_element_type=F32
    )
    value, slope = gelu_pair(pre[...].astype(F32))
    out[...] = (gate[...] * raw * slope).astype(BF)
    score[0] = jnp.sum(value * raw, axis=1, keepdims=True)


def raw_blocks(scalars, rows, gate, pre, a_whole, own, right, far, left):
    slots, width = rows.shape
    hid = pre.shape[1]
    block, step = hid // NZ, slots // RAW_STEPS
    n_rows = block // NX
    extra = a_whole.shape[2] - n_rows
    piece = (1, *own.shape[1:])
    here = pl.BlockSpec(piece, lambda p, i, sc: (p, 0, 0))
    return pl.pallas_call(
        raw_kernel,
        name="raw",
        out_shape=(
            jax.ShapeDtypeStruct((slots, hid), BF),
            jax.ShapeDtypeStruct((NZ * NX * extra, width), BF),
            jax.ShapeDtypeStruct((NZ, slots, 1), F32),
        ),
        grid_spec=pltpu.PrefetchScalarGridSpec(
            num_scalar_prefetch=1,
            grid=(NZ, RAW_STEPS),
            in_specs=[
                pl.BlockSpec((step, width), lambda p, i, sc: (i, 0)),
                pl.BlockSpec((step, 1), lambda p, i, sc: (i, 0)),
                pl.BlockSpec((step, block), lambda p, i, sc: (i, sc[p])),
                pl.BlockSpec((1, *a_whole.shape[1:]), lambda p, i, sc: (sc[p], 0, 0, 0)),
                here,
                here,
                pl.BlockSpec(piece, lambda p, i, sc: (jnp.minimum(p, NZ // 2 - 1), 0, 0)),
                pl.BlockSpec(piece, lambda p, i, sc: (jnp.maximum(p - NZ // 2, 0), 0, 0)),
                here,
            ],
            out_specs=(
                pl.BlockSpec((step, block), lambda p, i, sc: (i, sc[p])),
                pl.BlockSpec((NX * extra, width), lambda p, i, sc: (sc[p], 0)),
                pl.BlockSpec((1, step, 1), lambda p, i, sc: (p, i, 0)),
            ),
            scratch_shapes=[pltpu.VMEM((block, width), BF), pltpu.VMEM((NX * extra, width), F32)],
        ),
        compiler_params=pltpu.CompilerParams(vmem_limit_bytes=24 << 20),
        cost_estimate=pl.CostEstimate(
            flops=2 * slots * hid * width, bytes_accessed=22_000_000, transcendentals=slots * hid
        ),
    )(scalars, rows, gate, pre, a_whole, own, right, *far, left)


def to_all(a, axis, n):
    many = jnp.broadcast_to(a[None], (n, *a.shape))
    return lax.all_to_all(many, axis, 0, 0, tiled=True)


def body(grad_out, expert_ids, gates, routed_pre, routed_down, shared_pre, shared_down):
    z, x, y, c = (lax.axis_index(a) for a in ("z", "x", "y", "c"))
    owner = y * NC + c
    n_exp = NY * NC
    tok, width = grad_out.shape
    slots = routed_pre.shape[2]
    cap = slots // n_exp

    shard = jnp.concatenate([routed_down[0], shared_down], axis=0)
    half = width // 2
    a_whole = lax.all_gather(shard[:, :half], DP)
    a_whole = a_whole.reshape(NZ, NX, *a_whole.shape[1:])
    right, far, left = ring_gather(shard[:, half:], "z", 1)
    b_column = jnp.stack([*right, jnp.concatenate(far, axis=1), *left], axis=0)
    b_pieces = ring_gather(b_column, "x", 0)

    metas = jnp.concatenate([gates.astype(BF).T, expert_ids.astype(BF).T], axis=0)
    metas = jnp.pad(metas, ((0, 8 - metas.shape[0]), (0, width - tok)))
    mine = to_all(jnp.concatenate([grad_out, metas], axis=0), "y", NY)
    partner = hop(mine, "c", 1)

    pre = routed_pre[0, 0]
    hidden_b = gelu_pair(pre.astype(F32))[0].astype(BF)
    shared_b = gelu_pair(shared_pre.astype(F32))[0].astype(BF)

    scalars = jnp.stack([owner, c]).astype(jnp.int32)
    group_rows, recv_rows, scaled, gate_col = dispatch(scalars, mine, partner, tok, slots)

    shared_term = lax.dot_general(
        shared_b, group_rows, (((0,), (0,)), ((), ())), preferred_element_type=F32
    ).astype(BF)
    ta, tb = terms(hidden_b, scaled, shared_term.reshape(NZ, NX, -1, width))

    sum_a = lax.psum_scatter(ta.reshape(-1, half), "z", scatter_dimension=0, tiled=True)
    sum_a = lax.psum_scatter(sum_a, "x", scatter_dimension=0, tiled=True)
    sum_a = sum_a.astype(F32)

    def along(t, place, n):
        return lambda r: lax.dynamic_index_in_dim(t, (place + r) % n, 0, keepdims=False)

    sum_b = sum_ring(along(tb, x, NX), NX, "x", 0).astype(BF)
    sum_b = sum_ring(along(sum_b, z, NZ), NZ, "z", 1)
    total = jnp.concatenate([sum_a, sum_b], axis=1)
    rows = routed_down.shape[1]

    sc = jnp.stack([(z + (NZ - j)) % NZ for j in range(NZ)] + [x]).astype(jnp.int32)
    (own, right), far, (left,) = b_pieces
    routed_pre_grad, whole_shared, score = raw_blocks(
        sc, recv_rows, gate_col, pre, a_whole, own, right, far, left
    )
    slot_score = score.sum(axis=0)
    returned = lax.all_to_all(slot_score.reshape(n_exp, cap), EXPERT, 0, 0, tiled=True)

    own_ids = lax.optimization_barrier((expert_ids, gate_col))[0]
    labels = jnp.arange(n_exp, dtype=jnp.int32)
    onehot = own_ids[:, :, None] == labels[None, None, :]
    named = jnp.any(onehot, axis=1).astype(F32)
    order = jnp.arange(tok, dtype=jnp.int32)
    tri = (order[None, :] < order[:, None]).astype(F32)
    counts = lax.dot_general(tri, named, (((1,), (0,)), ((), ())), preferred_element_type=F32)
    rank = jnp.sum(jnp.where(onehot, counts[:, None, :], 0.0), axis=2).astype(jnp.int32)
    slot = own_ids * cap + rank
    each = jnp.arange(slots, dtype=jnp.int32)
    gate_grad = jnp.sum(
        jnp.where(slot[:, :, None] == each[None, None, :], returned.reshape(1, 1, slots), 0.0), axis=2
    )

    raw_shared = lax.dot_general(
        group_rows, whole_shared, (((1,), (1,)), ((), ())), preferred_element_type=F32
    )
    shared_pre_grad = (raw_shared * gelu_pair(shared_pre.astype(F32))[1]).astype(BF)
    return (
        routed_pre_grad.reshape(routed_pre.shape),
        total[:rows].reshape(1, rows, width),
        shared_pre_grad,
        total[rows:],
        gate_grad,
    )


def solution(mesh):
    split = Mesh(mesh.devices.reshape(NZ, NX, NY, NC), ("z", "x", "y", "c"))
    placed = (
        P(DP_EXPERT, None),
        P(DP_EXPERT, None),
        P(DP_EXPERT, None),
        P(DP, EXPERT, None, None),
        P(EXPERT, DP, None),
        P(DP, EXPERT),
        P(EXPERT_DP, None),
    )
    return jax.shard_map(
        body,
        mesh=split,
        in_specs=placed,
        out_specs=(
            P(DP, EXPERT, None, None),
            P(EXPERT, DP, None),
            P(DP, EXPERT),
            P(EXPERT_DP, None),
            P(DP_EXPERT, None),
        ),
        check_vma=False,
    )
```

```python
import jax
import jax.numpy as jnp
from jax import lax
from jax.experimental import pallas as pl
from jax.experimental.pallas import tpu as pltpu
from jax.sharding import Mesh
from jax.sharding import PartitionSpec as P


DP = ("z", "x")
EXPERT = ("y", "c")
DP_EXPERT = ("z", "x", "y", "c")
EXPERT_DP = ("y", "c", "z", "x")
NZ, NX, NY, NC = 8, 4, 4, 2


SQRT_TWO_PI = 0.7978845608028654
BF = jnp.bfloat16
F32 = jnp.float32


def hop(a, axis, by):
    n = lax.axis_size(axis)
    return lax.ppermute(a, axis, [(i, (i + by) % n) for i in range(n)])


def gelu_pair(inputs):
    cubic = inputs * inputs * inputs
    tangent = jnp.tanh(SQRT_TWO_PI * (inputs + 0.044715 * cubic))
    value = 0.5 * inputs * (1.0 + tangent)
    slope = 0.5 * (1.0 + tangent) + 0.5 * inputs * (1.0 - tangent * tangent) * SQRT_TWO_PI * (
        1.0 + 3.0 * 0.044715 * inputs * inputs
    )
    return (value, slope)


def added(a, b):
    return (a.astype(F32) + b.astype(F32)).astype(BF)


def ring_gather(a, axis, dim):
    n = lax.axis_size(axis)
    half = a.shape[dim] // 2
    right, left = [a], [a]
    for _ in range(1, n // 2):
        right.append(hop(right[-1], axis, 1))
        left.append(hop(left[-1], axis, -1))
    first = lax.slice_in_dim(right[-1], 0, half, axis=dim)
    second = lax.slice_in_dim(left[-1], half, 2 * half, axis=dim)
    far = (hop(first, axis, 1), hop(second, axis, -1))
    return right, far, left[:0:-1]


def sum_ring(block, n, axis, dim):
    far = block(n // 2)
    half = far.shape[dim] // 2
    first = lax.slice_in_dim(far, 0, half, axis=dim)
    second = lax.slice_in_dim(far, half, 2 * half, axis=dim)
    right = hop(first, axis, 1)
    left = hop(second, axis, -1)
    for k, r in enumerate(range(n // 2 - 1, 0, -1)):
        right, left = lax.optimization_barrier((right, left))
        if k == 0:
            grown = [(0, 0)] * far.ndim
            grown[dim] = (0, half)
            right = jnp.pad(right, grown)
            grown[dim] = (half, 0)
            left = jnp.pad(left, grown)
        right = hop(added(block(r), right), axis, 1)
        left = hop(added(block(n - r), left), axis, -1)
    right, left = lax.optimization_barrier((right, left))
    return block(0).astype(F32) + right.astype(F32) + left.astype(F32)


def dispatch_kernel(sc, mine, partner, grp, recv, scal, gate):
    owner, core = sc[0], sc[1]
    tok, cap = grp.shape[0] // 2, recv.shape[0] // 2
    me = owner.astype(F32)
    earlier = lax.broadcasted_iota(jnp.int32, (tok, tok), 0)
    later = lax.broadcasted_iota(jnp.int32, (tok, tok), 1)
    tri = jnp.where(earlier < later, 1.0, 0.0).astype(BF)
    place = lax.broadcasted_iota(jnp.int32, (cap, tok), 0)
    for ref, at in ((mine, core), (partner, 1 - core)):
        tokens = ref[0, :tok, :]
        meta = ref[0, tok:, :tok].astype(F32)
        g0, g1, i0, i1 = (meta[k : k + 1, :] for k in range(4))
        hit0, hit1 = (i0 == me), (i1 == me)
        named = jnp.where(hit0, 1.0, jnp.where(hit1, 1.0, 0.0))
        picked = jnp.where(hit0, g0, jnp.where(hit1, g1, 0.0))
        rank = lax.dot_general(
            jnp.broadcast_to(named, (8, tok)).astype(BF),
            tri,
            (((1,), (0,)), ((), ())),
            preferred_element_type=F32,
        )[0:1]
        rank = jnp.where(named > 0.0, rank, -1.0).astype(jnp.int32)
        onehot = jnp.where(place == rank, 1.0, 0.0)
        rows = lax.dot_general(
            onehot.astype(BF), tokens, (((1,), (0,)), ((), ())), preferred_element_type=F32
        )
        weight = jnp.sum(onehot * picked, axis=1, keepdims=True)
        grp[pl.ds(pl.multiple_of(at * tok, tok), tok), :] = tokens
        slot = pl.ds(pl.multiple_of(at * cap, cap), cap)
        recv[slot, :] = rows.astype(BF)
        scal[slot, :] = (weight * rows).astype(BF)
        gate[slot, :] = weight


def dispatch(scalars, mine, partner, tok, slots):
    width = mine.shape[2]
    cap2 = slots // NY
    taken = pl.BlockSpec((1, *mine.shape[1:]), lambda k: (k, 0, 0))

    def given(rows, cols):
        return pl.BlockSpec((rows, cols), lambda k: (k, 0))

    return pl.pallas_call(
        dispatch_kernel,
        name="dispatch",
        grid=(NY,),
        out_shape=(
            jax.ShapeDtypeStruct((NY * NC * tok, width), BF),
            jax.ShapeDtypeStruct((slots, width), BF),
            jax.ShapeDtypeStruct((slots, width), BF),
            jax.ShapeDtypeStruct((slots, 1), F32),
        ),
        in_specs=[pl.BlockSpec(memory_space=pltpu.SMEM), taken, taken],
        out_specs=(given(NC * tok, width), given(cap2, width), given(cap2, width), given(cap2, 1)),
        compiler_params=pltpu.CompilerParams(vmem_limit_bytes=24 << 20),
        cost_estimate=pl.CostEstimate(flops=200_000_000, bytes_accessed=10_000_000, transcendentals=0),
    )(scalars, mine, partner)


def terms_kernel(hidden, scal, tsh, ta, tb):
    out = lax.dot_general(
        hidden[...], scal[...], (((0,), (0,)), ((), ())), preferred_element_type=F32
    )
    nx, half = ta.shape[1], ta.shape[3]
    rows = hidden.shape[1] // nx
    out = out.astype(BF).reshape(nx, rows, 2 * half)
    ta[0, :, :rows, :] = out[:, :, :half]
    tb[:, 0, :rows, :] = out[:, :, half:]
    ta[0, :, rows:, :] = tsh[0, :, :, :half]
    tb[:, 0, rows:, :] = tsh[0, :, :, half:]


def terms(hidden, scal, tsh):
    slots, hid = hidden.shape
    width = scal.shape[1]
    rows, extra = hid // (NZ * NX), tsh.shape[2]
    tail = (rows + extra, width // 2)
    return pl.pallas_call(
        terms_kernel,
        name="terms",
        grid=(NZ,),
        out_shape=(
            jax.ShapeDtypeStruct((NZ, NX, *tail), BF),
            jax.ShapeDtypeStruct((NX, NZ, *tail), BF),
        ),
        in_specs=[
            pl.BlockSpec((slots, hid // NZ), lambda k: (0, k)),
            pl.BlockSpec((slots, width), lambda k: (0, 0)),
            pl.BlockSpec((1, NX, extra, width), lambda k: (k, 0, 0, 0)),
        ],
        out_specs=(
            pl.BlockSpec((1, NX, *tail), lambda k: (k, 0, 0, 0)),
            pl.BlockSpec((NX, 1, *tail), lambda k: (0, k, 0, 0)),
        ),
        compiler_params=pltpu.CompilerParams(vmem_limit_bytes=24 << 20),
        cost_estimate=pl.CostEstimate(
            flops=2 * slots * hid * width, bytes_accessed=20_000_000, transcendentals=0
        ),
    )(hidden, scal, tsh)


RAW_STEPS = 3
THIRD = 512


def raw_kernel(sc, rows, gate, pre, a_ref, own, right, far0, far1, left, *refs):
    *f_refs, out, wsh, score, whole, small = refs
    n_rows = whole.shape[0] // NX
    extra = small.shape[0] // NX
    x = sc[NZ]
    part = a_ref.shape[3]
    mid, last = slice(part, 2 * part), slice(2 * part, 3 * part)

    def put(value, r, cols):
        source = (x + (NX - r)) % NX
        at = pl.ds(pl.multiple_of(source * n_rows, n_rows), n_rows)
        whole[at, cols] = value[:n_rows]
        at = pl.ds(pl.multiple_of(source * extra, extra), extra)
        small[at, cols] = value[n_rows:].astype(F32)

    p = pl.program_id(0)

    @pl.when(pl.program_id(1) == 0)
    def _():
        for k in range(NX):
            whole[k * n_rows : (k + 1) * n_rows, :part] = a_ref[0, k, :n_rows, :]
            small[k * extra : (k + 1) * extra, :part] = a_ref[0, k, n_rows:, :].astype(F32)
        put(own[0], 0, mid)
        put(right[0], 1, mid)
        put(left[0], 3, mid)
        low = p < NZ // 2

        @pl.when(low)
        def _():
            put(far0[0], 2, mid)

        @pl.when(jnp.logical_not(low))
        def _():
            put(far1[0], 2, mid)

        for j in range(NZ):

            @pl.when(p == j)
            def _():
                for k in range(NX):
                    if j < NZ // 2:
                        put(f_refs[j][k], k, last)
                    elif j > NZ // 2:
                        put(f_refs[j + 1][k], k, last)
                    else:
                        put(f_refs[j + k // 2][k % 2], k, last)

        wsh[...] = small[...].astype(BF)

    raw = lax.dot_general(
        rows[...], whole[...], (((1,), (1,)), ((), ())), preferred_element_type=F32
    )
    value, slope = gelu_pair(pre[...].astype(F32))
    out[...] = (gate[...] * raw * slope).astype(BF)
    score[0] = jnp.sum(value * raw, axis=1, keepdims=True)


def raw_blocks(scalars, rows, gate, pre, a_whole, own, right, far, left, f_list):
    slots, width = rows.shape
    hid = pre.shape[1]
    block, step = hid // NZ, slots // RAW_STEPS
    n_rows = block // NX
    extra = a_whole.shape[2] - n_rows
    piece = (1, *own.shape[1:])
    here = pl.BlockSpec(piece, lambda p, i, sc: (p, 0, 0))
    once = pl.Buffered(1)
    return pl.pallas_call(
        raw_kernel,
        name="raw",
        out_shape=(
            jax.ShapeDtypeStruct((slots, hid), BF),
            jax.ShapeDtypeStruct((NZ * NX * extra, width), BF),
            jax.ShapeDtypeStruct((NZ, slots, 1), F32),
        ),
        grid_spec=pltpu.PrefetchScalarGridSpec(
            num_scalar_prefetch=1,
            grid=(NZ, RAW_STEPS),
            in_specs=[
                pl.BlockSpec((step, width), lambda p, i, sc: (i, 0)),
                pl.BlockSpec((step, 1), lambda p, i, sc: (i, 0)),
                pl.BlockSpec((step, block), lambda p, i, sc: (i, sc[p])),
                pl.BlockSpec((1, *a_whole.shape[1:]), lambda p, i, sc: (sc[p], 0, 0, 0)),
                here,
                here,
                pl.BlockSpec(piece, lambda p, i, sc: (jnp.minimum(p, NZ // 2 - 1), 0, 0)),
                pl.BlockSpec(piece, lambda p, i, sc: (jnp.maximum(p - NZ // 2, 0), 0, 0)),
                here,
            ]
            + [pl.BlockSpec(f.shape, lambda p, i, sc: (0, 0, 0), pipeline_mode=once) for f in f_list],
            out_specs=(
                pl.BlockSpec((step, block), lambda p, i, sc: (i, sc[p])),
                pl.BlockSpec((NX * extra, width), lambda p, i, sc: (sc[p], 0)),
                pl.BlockSpec((1, step, 1), lambda p, i, sc: (p, i, 0)),
            ),
            scratch_shapes=[pltpu.VMEM((block, width), BF), pltpu.VMEM((NX * extra, width), F32)],
        ),
        compiler_params=pltpu.CompilerParams(vmem_limit_bytes=24 << 20),
        cost_estimate=pl.CostEstimate(
            flops=2 * slots * hid * width, bytes_accessed=22_000_000, transcendentals=slots * hid
        ),
    )(scalars, rows, gate, pre, a_whole, own, right, *far, left, *f_list)


def to_all(a, axis, n):
    many = jnp.broadcast_to(a[None], (n, *a.shape))
    return lax.all_to_all(many, axis, 0, 0, tiled=True)


def body(grad_out, expert_ids, gates, routed_pre, routed_down, shared_pre, shared_down):
    z, x, y, c = (lax.axis_index(a) for a in ("z", "x", "y", "c"))
    owner = y * NC + c
    n_exp = NY * NC
    tok, width = grad_out.shape
    slots = routed_pre.shape[2]
    cap = slots // n_exp

    shard = jnp.concatenate([routed_down[0], shared_down], axis=0)
    half = width // 2
    half = width // 2
    a_whole = lax.all_gather(shard[:, :THIRD], DP)
    a_whole = a_whole.reshape(NZ, NX, *a_whole.shape[1:])
    right, far, left = ring_gather(shard[:, THIRD : 2 * THIRD], "z", 1)
    column = jnp.stack([*right, jnp.concatenate(far, axis=1), *left], axis=0)
    b_pieces = ring_gather(column, "x", 0)
    last = shard[:, 2 * THIRD :]
    line = jnp.stack([last] + [hop(last, "x", k) for k in range(1, NX)], axis=0)
    f_right, f_far, f_left = ring_gather(line, "z", 0)

    metas = jnp.concatenate([gates.astype(BF).T, expert_ids.astype(BF).T], axis=0)
    metas = jnp.pad(metas, ((0, 8 - metas.shape[0]), (0, width - tok)))
    mine = to_all(jnp.concatenate([grad_out, metas], axis=0), "y", NY)
    partner = hop(mine, "c", 1)

    pre = routed_pre[0, 0]
    hidden_b = gelu_pair(pre.astype(F32))[0].astype(BF)
    shared_b = gelu_pair(shared_pre.astype(F32))[0].astype(BF)

    scalars = jnp.stack([owner, c]).astype(jnp.int32)
    group_rows, recv_rows, scaled, gate_col = dispatch(scalars, mine, partner, tok, slots)

    shared_term = lax.dot_general(
        shared_b, group_rows, (((0,), (0,)), ((), ())), preferred_element_type=F32
    ).astype(BF)
    ta, tb = terms(hidden_b, scaled, shared_term.reshape(NZ, NX, -1, width))

    sum_a = lax.psum_scatter(ta.reshape(-1, half), "z", scatter_dimension=0, tiled=True)
    sum_a = lax.psum_scatter(sum_a, "x", scatter_dimension=0, tiled=True)
    sum_a = sum_a.astype(F32)

    def along(t, place, n):
        return lambda r: lax.dynamic_index_in_dim(t, (place + r) % n, 0, keepdims=False)

    sum_b = sum_ring(along(tb, x, NX), NX, "x", 0).astype(BF)
    sum_b = sum_ring(along(sum_b, z, NZ), NZ, "z", 1)
    total = jnp.concatenate([sum_a, sum_b], axis=1)
    rows = routed_down.shape[1]

    sc = jnp.stack([(z + (NZ - j)) % NZ for j in range(NZ)] + [x]).astype(jnp.int32)
    (own, right), far, (left,) = b_pieces
    routed_pre_grad, whole_shared, score = raw_blocks(
        sc, recv_rows, gate_col, pre, a_whole, own, right, far, left, [*f_right, *f_far, *f_left]
    )
    slot_score = score.sum(axis=0)
    returned = lax.all_to_all(slot_score.reshape(n_exp, cap), EXPERT, 0, 0, tiled=True)

    own_ids = lax.optimization_barrier((expert_ids, gate_col))[0]
    labels = jnp.arange(n_exp, dtype=jnp.int32)
    onehot = own_ids[:, :, None] == labels[None, None, :]
    named = jnp.any(onehot, axis=1).astype(F32)
    order = jnp.arange(tok, dtype=jnp.int32)
    tri = (order[None, :] < order[:, None]).astype(F32)
    counts = lax.dot_general(tri, named, (((1,), (0,)), ((), ())), preferred_element_type=F32)
    rank = jnp.sum(jnp.where(onehot, counts[:, None, :], 0.0), axis=2).astype(jnp.int32)
    slot = own_ids * cap + rank
    each = jnp.arange(slots, dtype=jnp.int32)
    gate_grad = jnp.sum(
        jnp.where(slot[:, :, None] == each[None, None, :], returned.reshape(1, 1, slots), 0.0), axis=2
    )

    raw_shared = lax.dot_general(
        group_rows, whole_shared, (((1,), (1,)), ((), ())), preferred_element_type=F32
    )
    shared_pre_grad = (raw_shared * gelu_pair(shared_pre.astype(F32))[1]).astype(BF)
    return (
        routed_pre_grad.reshape(routed_pre.shape),
        total[:rows].reshape(1, rows, width),
        shared_pre_grad,
        total[rows:],
        gate_grad,
    )


def solution(mesh):
    split = Mesh(mesh.devices.reshape(NZ, NX, NY, NC), ("z", "x", "y", "c"))
    placed = (
        P(DP_EXPERT, None),
        P(DP_EXPERT, None),
        P(DP_EXPERT, None),
        P(DP, EXPERT, None, None),
        P(EXPERT, DP, None),
        P(DP, EXPERT),
        P(EXPERT_DP, None),
    )
    return jax.shard_map(
        body,
        mesh=split,
        in_specs=placed,
        out_specs=(
            P(DP, EXPERT, None, None),
            P(EXPERT, DP, None),
            P(DP, EXPERT),
            P(EXPERT_DP, None),
            P(DP_EXPERT, None),
        ),
        check_vma=False,
    )
```

```python
import jax
import jax.numpy as jnp
from jax import lax
from jax.experimental import pallas as pl
from jax.experimental.pallas import tpu as pltpu
from jax.sharding import Mesh
from jax.sharding import PartitionSpec as P


DP = ("z", "x")
EXPERT = ("y", "c")
DP_EXPERT = ("z", "x", "y", "c")
EXPERT_DP = ("y", "c", "z", "x")
NZ, NX, NY, NC = 8, 4, 4, 2


SQRT_TWO_PI = 0.7978845608028654
BF = jnp.bfloat16
F32 = jnp.float32


def hop(a, axis, by):
    n = lax.axis_size(axis)
    return lax.ppermute(a, axis, [(i, (i + by) % n) for i in range(n)])


def gelu_pair(inputs):
    cubic = inputs * inputs * inputs
    tangent = jnp.tanh(SQRT_TWO_PI * (inputs + 0.044715 * cubic))
    value = 0.5 * inputs * (1.0 + tangent)
    slope = 0.5 * (1.0 + tangent) + 0.5 * inputs * (1.0 - tangent * tangent) * SQRT_TWO_PI * (
        1.0 + 3.0 * 0.044715 * inputs * inputs
    )
    return (value, slope)


def added(a, b):
    return (a.astype(F32) + b.astype(F32)).astype(BF)


def ring_gather(a, axis, dim):
    n = lax.axis_size(axis)
    half = a.shape[dim] // 2
    right, left = [a], [a]
    for _ in range(1, n // 2):
        right.append(hop(right[-1], axis, 1))
        left.append(hop(left[-1], axis, -1))
    first = lax.slice_in_dim(right[-1], 0, half, axis=dim)
    second = lax.slice_in_dim(left[-1], half, 2 * half, axis=dim)
    far = (hop(first, axis, 1), hop(second, axis, -1))
    return right, far, left[:0:-1]


def sum_ring(block, n, axis, dim):
    far = block(n // 2)
    half = far.shape[dim] // 2
    first = lax.slice_in_dim(far, 0, half, axis=dim)
    second = lax.slice_in_dim(far, half, 2 * half, axis=dim)
    right = hop(first, axis, 1)
    left = hop(second, axis, -1)
    for k, r in enumerate(range(n // 2 - 1, 0, -1)):
        right, left = lax.optimization_barrier((right, left))
        if k == 0:
            grown = [(0, 0)] * far.ndim
            grown[dim] = (0, half)
            right = jnp.pad(right, grown)
            grown[dim] = (half, 0)
            left = jnp.pad(left, grown)
        right = hop(added(block(r), right), axis, 1)
        left = hop(added(block(n - r), left), axis, -1)
    right, left = lax.optimization_barrier((right, left))
    return block(0).astype(F32) + right.astype(F32) + left.astype(F32)


def dispatch_kernel(sc, mine, partner, grp, recv, scal, gate):
    owner, core = sc[0], sc[1]
    tok, cap = grp.shape[0] // 2, recv.shape[0] // 2
    me = owner.astype(F32)
    earlier = lax.broadcasted_iota(jnp.int32, (tok, tok), 0)
    later = lax.broadcasted_iota(jnp.int32, (tok, tok), 1)
    tri = jnp.where(earlier < later, 1.0, 0.0).astype(BF)
    place = lax.broadcasted_iota(jnp.int32, (cap, tok), 0)
    for ref, at in ((mine, core), (partner, 1 - core)):
        tokens = ref[0, :tok, :]
        meta = ref[0, tok:, :tok].astype(F32)
        g0, g1, i0, i1 = (meta[k : k + 1, :] for k in range(4))
        hit0, hit1 = (i0 == me), (i1 == me)
        named = jnp.where(hit0, 1.0, jnp.where(hit1, 1.0, 0.0))
        picked = jnp.where(hit0, g0, jnp.where(hit1, g1, 0.0))
        rank = lax.dot_general(
            jnp.broadcast_to(named, (8, tok)).astype(BF),
            tri,
            (((1,), (0,)), ((), ())),
            preferred_element_type=F32,
        )[0:1]
        rank = jnp.where(named > 0.0, rank, -1.0).astype(jnp.int32)
        onehot = jnp.where(place == rank, 1.0, 0.0)
        rows = lax.dot_general(
            onehot.astype(BF), tokens, (((1,), (0,)), ((), ())), preferred_element_type=F32
        )
        weight = jnp.sum(onehot * picked, axis=1, keepdims=True)
        grp[pl.ds(pl.multiple_of(at * tok, tok), tok), :] = tokens
        slot = pl.ds(pl.multiple_of(at * cap, cap), cap)
        recv[slot, :] = rows.astype(BF)
        scal[slot, :] = (weight * rows).astype(BF)
        gate[slot, :] = weight


def dispatch(scalars, mine, partner, tok, slots):
    width = mine.shape[2]
    cap2 = slots // NY
    taken = pl.BlockSpec((1, *mine.shape[1:]), lambda k: (k, 0, 0))

    def given(rows, cols):
        return pl.BlockSpec((rows, cols), lambda k: (k, 0))

    return pl.pallas_call(
        dispatch_kernel,
        name="dispatch",
        grid=(NY,),
        out_shape=(
            jax.ShapeDtypeStruct((NY * NC * tok, width), BF),
            jax.ShapeDtypeStruct((slots, width), BF),
            jax.ShapeDtypeStruct((slots, width), BF),
            jax.ShapeDtypeStruct((slots, 1), F32),
        ),
        in_specs=[pl.BlockSpec(memory_space=pltpu.SMEM), taken, taken],
        out_specs=(given(NC * tok, width), given(cap2, width), given(cap2, width), given(cap2, 1)),
        compiler_params=pltpu.CompilerParams(vmem_limit_bytes=24 << 20),
        cost_estimate=pl.CostEstimate(flops=200_000_000, bytes_accessed=10_000_000, transcendentals=0),
    )(scalars, mine, partner)


def terms_kernel(hidden, scal, tsh, ta, tb):
    out = lax.dot_general(
        hidden[...], scal[...], (((0,), (0,)), ((), ())), preferred_element_type=F32
    )
    nx, half = ta.shape[1], ta.shape[3]
    rows = hidden.shape[1] // nx
    out = out.astype(BF).reshape(nx, rows, 2 * half)
    ta[0, :, :rows, :] = out[:, :, :half]
    tb[:, 0, :rows, :] = out[:, :, half:]
    ta[0, :, rows:, :] = tsh[0, :, :, :half]
    tb[:, 0, rows:, :] = tsh[0, :, :, half:]


def terms(hidden, scal, tsh):
    slots, hid = hidden.shape
    width = scal.shape[1]
    rows, extra = hid // (NZ * NX), tsh.shape[2]
    tail = (rows + extra, width // 2)
    return pl.pallas_call(
        terms_kernel,
        name="terms",
        grid=(NZ,),
        out_shape=(
            jax.ShapeDtypeStruct((NZ, NX, *tail), BF),
            jax.ShapeDtypeStruct((NX, NZ, *tail), BF),
        ),
        in_specs=[
            pl.BlockSpec((slots, hid // NZ), lambda k: (0, k)),
            pl.BlockSpec((slots, width), lambda k: (0, 0)),
            pl.BlockSpec((1, NX, extra, width), lambda k: (k, 0, 0, 0)),
        ],
        out_specs=(
            pl.BlockSpec((1, NX, *tail), lambda k: (k, 0, 0, 0)),
            pl.BlockSpec((NX, 1, *tail), lambda k: (0, k, 0, 0)),
        ),
        compiler_params=pltpu.CompilerParams(vmem_limit_bytes=24 << 20),
        cost_estimate=pl.CostEstimate(
            flops=2 * slots * hid * width, bytes_accessed=20_000_000, transcendentals=0
        ),
    )(hidden, scal, tsh)


RAW_STEPS = 3


def raw_kernel(sc, rows, gate, pre, own, right, far0, far1, left, *refs):
    *f_refs, out, wsh, score, whole, small = refs
    n_rows = whole.shape[0] // NX
    extra = small.shape[0] // NX
    x = sc[NZ]
    part = own.shape[2]
    mid, last = slice(0, part), slice(part, 2 * part)

    def put(value, r, cols):
        source = (x + (NX - r)) % NX
        at = pl.ds(pl.multiple_of(source * n_rows, n_rows), n_rows)
        whole[at, cols] = value[:n_rows]
        at = pl.ds(pl.multiple_of(source * extra, extra), extra)
        small[at, cols] = value[n_rows:].astype(F32)

    p = pl.program_id(0)

    @pl.when(pl.program_id(1) == 0)
    def _():
        put(own[0], 0, mid)
        put(right[0], 1, mid)
        put(left[0], 3, mid)
        low = p < NZ // 2

        @pl.when(low)
        def _():
            put(far0[0], 2, mid)

        @pl.when(jnp.logical_not(low))
        def _():
            put(far1[0], 2, mid)

        for j in range(NZ):

            @pl.when(p == j)
            def _():
                for k in range(NX):
                    if j < NZ // 2:
                        put(f_refs[j][k], k, last)
                    elif j > NZ // 2:
                        put(f_refs[j + 1][k], k, last)
                    else:
                        put(f_refs[j + k // 2][k % 2], k, last)

        wsh[...] = small[...].astype(BF)

    raw = lax.dot_general(
        rows[...], whole[...], (((1,), (1,)), ((), ())), preferred_element_type=F32
    )
    value, slope = gelu_pair(pre[...].astype(F32))
    out[...] = (gate[...] * raw * slope).astype(BF)
    score[0] = jnp.sum(value * raw, axis=1, keepdims=True)


def raw_blocks(scalars, rows, gate, pre, own, right, far, left, f_list):
    slots, width = rows.shape
    hid = pre.shape[1]
    block, step = hid // NZ, slots // RAW_STEPS
    n_rows = block // NX
    extra = own.shape[1] - n_rows
    piece = (1, *own.shape[1:])
    here = pl.BlockSpec(piece, lambda p, i, sc: (p, 0, 0))
    once = pl.Buffered(1)
    return pl.pallas_call(
        raw_kernel,
        name="raw",
        out_shape=(
            jax.ShapeDtypeStruct((slots, hid), BF),
            jax.ShapeDtypeStruct((NZ * NX * extra, width), BF),
            jax.ShapeDtypeStruct((NZ, slots, 1), F32),
        ),
        grid_spec=pltpu.PrefetchScalarGridSpec(
            num_scalar_prefetch=1,
            grid=(NZ, RAW_STEPS),
            in_specs=[
                pl.BlockSpec((step, width), lambda p, i, sc: (i, 0)),
                pl.BlockSpec((step, 1), lambda p, i, sc: (i, 0)),
                pl.BlockSpec((step, block), lambda p, i, sc: (i, sc[p])),
                here,
                here,
                pl.BlockSpec(piece, lambda p, i, sc: (jnp.minimum(p, NZ // 2 - 1), 0, 0)),
                pl.BlockSpec(piece, lambda p, i, sc: (jnp.maximum(p - NZ // 2, 0), 0, 0)),
                here,
            ]
            + [pl.BlockSpec(f.shape, lambda p, i, sc: (0, 0, 0), pipeline_mode=once) for f in f_list],
            out_specs=(
                pl.BlockSpec((step, block), lambda p, i, sc: (i, sc[p])),
                pl.BlockSpec((NX * extra, width), lambda p, i, sc: (sc[p], 0)),
                pl.BlockSpec((1, step, 1), lambda p, i, sc: (p, i, 0)),
            ),
            scratch_shapes=[pltpu.VMEM((block, width), BF), pltpu.VMEM((NX * extra, width), F32)],
        ),
        compiler_params=pltpu.CompilerParams(vmem_limit_bytes=24 << 20),
        cost_estimate=pl.CostEstimate(
            flops=2 * slots * hid * width, bytes_accessed=22_000_000, transcendentals=slots * hid
        ),
    )(scalars, rows, gate, pre, own, right, *far, left, *f_list)


def to_all(a, axis, n):
    many = jnp.broadcast_to(a[None], (n, *a.shape))
    return lax.all_to_all(many, axis, 0, 0, tiled=True)


def body(grad_out, expert_ids, gates, routed_pre, routed_down, shared_pre, shared_down):
    z, x, y, c = (lax.axis_index(a) for a in ("z", "x", "y", "c"))
    owner = y * NC + c
    n_exp = NY * NC
    tok, width = grad_out.shape
    slots = routed_pre.shape[2]
    cap = slots // n_exp

    shard = jnp.concatenate([routed_down[0], shared_down], axis=0)
    half = width // 2
    half = width // 2
    half = width // 2
    right, far, left = ring_gather(shard[:, :half], "z", 1)
    column = jnp.stack([*right, jnp.concatenate(far, axis=1), *left], axis=0)
    b_pieces = ring_gather(column, "x", 0)
    last = shard[:, half:]
    line = jnp.stack([last] + [hop(last, "x", k) for k in range(1, NX)], axis=0)
    f_right, f_far, f_left = ring_gather(line, "z", 0)

    metas = jnp.concatenate([gates.astype(BF).T, expert_ids.astype(BF).T], axis=0)
    metas = jnp.pad(metas, ((0, 8 - metas.shape[0]), (0, width - tok)))
    mine = to_all(jnp.concatenate([grad_out, metas], axis=0), "y", NY)
    partner = hop(mine, "c", 1)

    pre = routed_pre[0, 0]
    hidden_b = gelu_pair(pre.astype(F32))[0].astype(BF)
    shared_b = gelu_pair(shared_pre.astype(F32))[0].astype(BF)

    scalars = jnp.stack([owner, c]).astype(jnp.int32)
    group_rows, recv_rows, scaled, gate_col = dispatch(scalars, mine, partner, tok, slots)

    shared_term = lax.dot_general(
        shared_b, group_rows, (((0,), (0,)), ((), ())), preferred_element_type=F32
    ).astype(BF)
    ta, tb = terms(hidden_b, scaled, shared_term.reshape(NZ, NX, -1, width))

    sum_a = lax.psum_scatter(ta.reshape(-1, half), "z", scatter_dimension=0, tiled=True)
    sum_a = lax.psum_scatter(sum_a, "x", scatter_dimension=0, tiled=True)
    sum_a = sum_a.astype(F32)

    def along(t, place, n):
        return lambda r: lax.dynamic_index_in_dim(t, (place + r) % n, 0, keepdims=False)

    sum_b = sum_ring(along(tb, x, NX), NX, "x", 0).astype(BF)
    sum_b = sum_ring(along(sum_b, z, NZ), NZ, "z", 1)
    total = jnp.concatenate([sum_a, sum_b], axis=1)
    rows = routed_down.shape[1]

    sc = jnp.stack([(z + (NZ - j)) % NZ for j in range(NZ)] + [x]).astype(jnp.int32)
    (own, right), far, (left,) = b_pieces
    routed_pre_grad, whole_shared, score = raw_blocks(
        sc, recv_rows, gate_col, pre, own, right, far, left, [*f_right, *f_far, *f_left]
    )
    slot_score = score.sum(axis=0)
    returned = lax.all_to_all(slot_score.reshape(n_exp, cap), EXPERT, 0, 0, tiled=True)

    own_ids = lax.optimization_barrier((expert_ids, gate_col))[0]
    labels = jnp.arange(n_exp, dtype=jnp.int32)
    onehot = own_ids[:, :, None] == labels[None, None, :]
    named = jnp.any(onehot, axis=1).astype(F32)
    order = jnp.arange(tok, dtype=jnp.int32)
    tri = (order[None, :] < order[:, None]).astype(F32)
    counts = lax.dot_general(tri, named, (((1,), (0,)), ((), ())), preferred_element_type=F32)
    rank = jnp.sum(jnp.where(onehot, counts[:, None, :], 0.0), axis=2).astype(jnp.int32)
    slot = own_ids * cap + rank
    each = jnp.arange(slots, dtype=jnp.int32)
    gate_grad = jnp.sum(
        jnp.where(slot[:, :, None] == each[None, None, :], returned.reshape(1, 1, slots), 0.0), axis=2
    )

    raw_shared = lax.dot_general(
        group_rows, whole_shared, (((1,), (1,)), ((), ())), preferred_element_type=F32
    )
    shared_pre_grad = (raw_shared * gelu_pair(shared_pre.astype(F32))[1]).astype(BF)
    return (
        routed_pre_grad.reshape(routed_pre.shape),
        total[:rows].reshape(1, rows, width),
        shared_pre_grad,
        total[rows:],
        gate_grad,
    )


def solution(mesh):
    split = Mesh(mesh.devices.reshape(NZ, NX, NY, NC), ("z", "x", "y", "c"))
    placed = (
        P(DP_EXPERT, None),
        P(DP_EXPERT, None),
        P(DP_EXPERT, None),
        P(DP, EXPERT, None, None),
        P(EXPERT, DP, None),
        P(DP, EXPERT),
        P(EXPERT_DP, None),
    )
    return jax.shard_map(
        body,
        mesh=split,
        in_specs=placed,
        out_specs=(
            P(DP, EXPERT, None, None),
            P(EXPERT, DP, None),
            P(DP, EXPERT),
            P(EXPERT_DP, None),
            P(DP_EXPERT, None),
        ),
        check_vma=False,
    )
```
